128 devices in a mesh: req: 16 (over z, x_lo, core), blk: 8 (over y, x_hi).
Axes of the slice: x: 4 (x_hi: 2, x_lo: 2; x = x_hi * 2 + x_lo), y: 4, z: 4, core: 2. Of those that a mesh axis runs over, the one named last changes fastest.
Arguments:
- prefill_rows: bfloat16 [8, 16, 256, 1536], P('blk', 'req'), may hold values from -3 to 3
- decode_rows: bfloat16 [8, 16, 16, 1536], P('blk', 'req'), may hold values from -3 to 3
- cache_pool: bfloat16 [8, 16, 408, 16, 512], P('blk', 'req'), may hold values from -300 to 300
- page_table: int32 [8, 16, 17, 24], P('blk', 'req'), may hold values from 0 to 407, as said below
- lengths: int32 [8, 16, 17], P('blk', 'req'), may hold values from 1 to 383, as said below
- destination: int32 [8, 16, 16], P('blk', 'req'), may hold values from 0 to 15, as said below
- attn_gain: bfloat16 [1536], replicated, may hold values from 0.5 to 1.5
- inproj_weight: bfloat16 [1536, 2048], replicated, may hold values from -0.15625 to 0.15625
- inproj_bias: bfloat16 [2048], replicated, may hold values from -3 to 3
- outproj_weight: bfloat16 [1536, 1536], replicated, may hold values from -0.15625 to 0.15625
- mlp_gain: bfloat16 [1536], replicated, may hold values from 0.5 to 1.5
- gate_up: bfloat16 [1536, 2, 8960], P('req', None, 'blk'), may hold values from -0.15625 to 0.15625
- down_weight: bfloat16 [8960, 1536], P('blk', 'req'), may hold values from -0.0625 to 0.0625
Outputs:
- prefill_out: bfloat16 [8, 16, 256, 1536], P('blk', 'req')
- decode_out: bfloat16 [8, 16, 16, 1536], P('blk', 'req')
- new_cache: bfloat16 [8, 16, 16, 384, 512], P('blk', 'req')
The draws below stay inside these ranges and needn't reach their ends.
Inputs may be any that keep to these rules, and one draw needn't show every extreme that they name: Each device sends exactly 0 or 2 of its decode requests to each index of req and receives exactly 16; destination minus source index, modulo the size of req, depends only on the blk index and the slot. `lengths`: slot 16 is the prefill request's context. Every device holds a decode request of length 383. `page_table`: on each device a permutation of its 408 pages.
All inputs are finite; a program needn't handle non-finite values.
Results may differ from the reference program's by a relative error of at most 0.024.
Values may be sent and summed in bfloat16 or wider, within the bound.
A program may use at most 192 MiB of HBM per device.

```python
import math
import jax
import jax.numpy as jnp
from jax import lax

D = 1536
QUERY_HEADS = 12
KEY_VALUE_HEADS = 2
HEAD_SIZE = 128
FF = 8960
PAGE = 16
MAXP = 24
DEC_DEV = 16
CAP = 2
PRE_DEV = 256
KVW = 512
N_REQ = 16
N_BLK = 8


def draw_cache_pool(key, part):
    page_total = (DEC_DEV + 1) * MAXP
    width_per_row = 2 * KEY_VALUE_HEADS * HEAD_SIZE
    pool_shape = (N_BLK, N_REQ, page_total * PAGE, width_per_row)
    base_draw = jnp.clip(jax.random.normal(key, pool_shape, jnp.float32), -6.0, 6.0)
    return base_draw.reshape(N_BLK, N_REQ, page_total, PAGE, width_per_row).astype(jnp.bfloat16)


def draw_page_table(key, part):
    page_total = (DEC_DEV + 1) * MAXP
    device_keys = jax.random.split(key, N_BLK * N_REQ)
    perms = jax.vmap(lambda one_key: jax.random.permutation(one_key, page_total))(device_keys)
    return perms.reshape(N_BLK, N_REQ, DEC_DEV + 1, MAXP).astype(jnp.int32)


def draw_lengths(key, part):
    first_key, second_key, third_key = jax.random.split(key, 3)
    length_shape = (N_BLK, N_REQ, DEC_DEV + 1)
    first_draw = jax.random.randint(first_key, length_shape, 0, 1000)
    second_draw = jax.random.randint(second_key, length_shape, 0, 1000)
    length_span = MAXP * PAGE - 2
    base_draw = 1 + length_span * first_draw * second_draw // 999000
    forced = jax.random.randint(third_key, (N_BLK, N_REQ, 1), 0, DEC_DEV)
    slot_ids = jnp.arange(DEC_DEV + 1, dtype=jnp.int32)[None, None, :]
    return jnp.where(slot_ids == forced, MAXP * PAGE - 1, base_draw).astype(jnp.int32)


def draw_destination(key, part):
    column_keys = jax.random.split(key, N_BLK)

    def column_offsets(one_key):
        first_key, second_key = jax.random.split(one_key)
        picked_offsets = jax.random.permutation(first_key, N_REQ)[:DEC_DEV // CAP]
        slot_order = jax.random.permutation(second_key, DEC_DEV)
        return picked_offsets[slot_order // CAP]
    offsets = jax.vmap(column_offsets)(column_keys)
    source = jnp.arange(N_REQ, dtype=jnp.int32)
    return ((source[None, :, None] + offsets[:, None, :]) % N_REQ).astype(jnp.int32)


def level_of(key, extent, cuts, smallest, high):
    level, own = 1.0, jax.random.fold_in(key, 6)
    for dim, parts in cuts:
        steps = jnp.exp(jax.random.uniform(jax.random.fold_in(own, dim), (parts,), jnp.float32, smallest / len(cuts), high / len(cuts)))
        level = level * jnp.repeat(steps, extent[dim] // parts).reshape([-1 if axis == dim else 1 for axis in range(len(extent))])
    return level


def scatter_about(own_key, shape, spread, bound, cuts=(), held_as=jnp.bfloat16):
    array = jax.random.normal(own_key, shape, jnp.float32) * spread
    if len(cuts) > 0:
        array = level_of(own_key, shape, cuts, -0.22, 0.18) * array
    return jnp.clip(array, min=-bound, max=bound).astype(held_as)


def setup_inputs(seed: int = 0) -> dict:
    keys = jax.random.split(jax.random.key(seed), 14)
    prefill_rows = scatter_about(keys[0], (N_BLK, N_REQ, PRE_DEV, D), 0.5, 3.0, ((0, 8), (1, 16)))
    decode_rows = scatter_about(keys[1], (N_BLK, N_REQ, DEC_DEV, D), 0.5, 3.0, ((0, 8), (1, 16)))
    cache_pool = draw_cache_pool(jax.random.fold_in(keys[13], 71), 0)
    page_table = draw_page_table(jax.random.fold_in(keys[13], 71), 0)
    lengths = draw_lengths(jax.random.fold_in(keys[13], 71), 0)
    destination = draw_destination(jax.random.fold_in(keys[13], 71), 0)
    attn_gain = jnp.clip(1.0 + 0.1 * jax.random.normal(keys[6], (D,), jnp.float32), 0.5, 1.5).astype(jnp.bfloat16)
    inproj_weight = scatter_about(keys[7], (D, QUERY_HEADS * HEAD_SIZE + KVW), D ** -0.5, 0.15625)
    inproj_bias = scatter_about(keys[8], (QUERY_HEADS * HEAD_SIZE + KVW,), 0.5, 3.0)
    outproj_weight = scatter_about(keys[9], (QUERY_HEADS * HEAD_SIZE, D), (QUERY_HEADS * HEAD_SIZE) ** -0.5, 0.15625)
    mlp_gain = jnp.clip(1.0 + 0.1 * jax.random.normal(keys[10], (D,), jnp.float32), 0.5, 1.5).astype(jnp.bfloat16)
    gate_up = scatter_about(keys[11], (D, 2, FF), D ** -0.5, 0.15625, ((0, 16), (2, 8)))
    down_weight = scatter_about(keys[12], (FF, D), FF ** -0.5, 0.0625, ((0, 8), (1, 16)))
    return dict(prefill_rows=prefill_rows, decode_rows=decode_rows, cache_pool=cache_pool, page_table=page_table, lengths=lengths, destination=destination, attn_gain=attn_gain, inproj_weight=inproj_weight, inproj_bias=inproj_bias, outproj_weight=outproj_weight, mlp_gain=mlp_gain, gate_up=gate_up, down_weight=down_weight)


rms_eps = 1e-06
rope_base = 1000000.0

def rms_scale(rows, gain_row):
    rows_wide = rows.astype(jnp.float32)
    inverse = lax.rsqrt(lax.optimization_barrier(jnp.mean(rows_wide * rows_wide, axis=-1, keepdims=True)) + rms_eps)
    return (rows_wide * inverse * gain_row.astype(jnp.float32)).astype(jnp.bfloat16)

def apply_rotary(vectors, token_positions):
    head_dim = vectors.shape[-1]
    half_dim = head_dim // 2
    frequency = rope_base ** (-2.0 * jnp.arange(half_dim, dtype=jnp.float32) / head_dim)
    angles = token_positions.astype(jnp.float32)[:, None] * frequency[None, :]
    cosine = jnp.concatenate([jnp.cos(angles), jnp.cos(angles)], axis=-1)[:, None, :]
    sine_table = jnp.concatenate([jnp.sin(angles), jnp.sin(angles)], axis=-1)[:, None, :]
    turned = jnp.concatenate([-vectors[..., half_dim:], vectors[..., :half_dim]], axis=-1)
    return vectors * cosine + turned * sine_table

def project(normed, weight, bias_row, token_positions):
    mixed_batch = jnp.dot(normed, weight, preferred_element_type=jnp.float32) + bias_row.astype(jnp.float32)
    query_head_width = QUERY_HEADS * HEAD_SIZE
    key_head_width = KEY_VALUE_HEADS * HEAD_SIZE
    query_rows = apply_rotary(mixed_batch[:, :query_head_width].reshape(-1, QUERY_HEADS, HEAD_SIZE), token_positions)
    key_row_block = apply_rotary(mixed_batch[:, query_head_width:query_head_width + key_head_width].reshape(-1, KEY_VALUE_HEADS, HEAD_SIZE), token_positions)
    value_rows = mixed_batch[:, query_head_width + key_head_width:]
    key_value_pair = jnp.concatenate([key_row_block.reshape(-1, key_head_width), value_rows], axis=-1)
    return (query_rows.reshape(-1, query_head_width).astype(jnp.bfloat16), key_value_pair.astype(jnp.bfloat16))

def attend(query_rows, key_value_pair, allowed):
    batch_count = query_rows.shape[0]
    total_rows = query_rows.shape[1]
    group_width = QUERY_HEADS // KEY_VALUE_HEADS
    key_head_width = KEY_VALUE_HEADS * HEAD_SIZE
    grouped_heads = query_rows.reshape(batch_count, total_rows, KEY_VALUE_HEADS, group_width, HEAD_SIZE).astype(jnp.float32)
    key_row_block = key_value_pair[:, :, :key_head_width].reshape(batch_count, -1, KEY_VALUE_HEADS, HEAD_SIZE).astype(jnp.float32)
    value_rows = key_value_pair[:, :, key_head_width:].reshape(batch_count, -1, KEY_VALUE_HEADS, HEAD_SIZE).astype(jnp.float32)
    scores = jnp.einsum('bqhgd,bkhd->bhgqk', grouped_heads, key_row_block, precision=lax.Precision.HIGHEST) / math.sqrt(HEAD_SIZE)
    scores = jnp.where(allowed[:, None, None, :, :], scores, -jnp.inf)
    row_max = lax.optimization_barrier(jnp.max(scores, axis=-1, keepdims=True))
    weights = jnp.exp(scores - row_max)
    weights = (weights / lax.optimization_barrier(jnp.sum(weights, axis=-1, keepdims=True))).astype(jnp.bfloat16)
    result = jnp.einsum('bhgqk,bkhd->bqhgd', weights.astype(jnp.float32), value_rows, precision=lax.Precision.HIGHEST)
    return result.reshape(batch_count, total_rows, QUERY_HEADS * HEAD_SIZE).astype(jnp.bfloat16)

def extend(cache_rows, key_value_pair, lengths_now):
    token_positions = jnp.arange(cache_rows.shape[1], dtype=jnp.int32)[None, :, None]
    limit = lengths_now[:, None, None]
    return jnp.where(token_positions < limit, cache_rows, jnp.where(token_positions == limit, key_value_pair[:, None, :], jnp.zeros_like(cache_rows)))

def blockwise_down(hidden, down_weight):
    block_width = FF // N_BLK
    hidden_blocks = hidden.reshape(hidden.shape[0], N_BLK, block_width).transpose(1, 0, 2)
    down_blocks = down_weight.reshape(N_BLK, block_width, -1)

    def one_block(block_args):
        hidden_one, down_one = block_args
        return jnp.dot(hidden_one, down_one, preferred_element_type=jnp.float32).astype(jnp.bfloat16)
    partial_value = lax.map(one_block, (hidden_blocks, down_blocks))
    partial_value = lax.optimization_barrier(partial_value)
    return lax.optimization_barrier(jnp.sum(partial_value.astype(jnp.float32), axis=0))

def device_layer(prefill_x, context, context_length, decode_x, decode_cache, decode_length, attn_gain, inproj_weight, inproj_bias, outproj_weight, mlp_gain, gate_up, down_weight):
    prefill_count = prefill_x.shape[0]
    cache_length = context.shape[0]
    block_ids = jnp.arange(prefill_count, dtype=jnp.int32)
    cache_ids = jnp.arange(cache_length, dtype=jnp.int32)
    prefill_q, prefill_kv = project(rms_scale(prefill_x, attn_gain), inproj_weight, inproj_bias, context_length + block_ids)
    key_block = jnp.concatenate([context, prefill_kv], axis=0)
    allowed = jnp.concatenate([jnp.broadcast_to(cache_ids[None, :] < context_length, (prefill_count, cache_length)), block_ids[None, :] <= block_ids[:, None]], axis=1)
    prefill_att = attend(prefill_q[None], key_block[None], allowed[None])[0]
    decode_q, decode_kv = project(rms_scale(decode_x, attn_gain), inproj_weight, inproj_bias, decode_length)
    cache_after = extend(decode_cache, decode_kv, decode_length)
    decode_allowed = (cache_ids[None, :] <= decode_length[:, None])[:, None, :]
    decode_att = attend(decode_q[:, None, :], cache_after, decode_allowed)[:, 0]
    inputs_all = jnp.concatenate([prefill_x, decode_x], axis=0)
    attended = jnp.concatenate([prefill_att, decode_att], axis=0)
    residual = inputs_all.astype(jnp.float32) + jnp.dot(attended, outproj_weight, preferred_element_type=jnp.float32)
    mlp_in = rms_scale(residual, mlp_gain)
    gate_rows = jnp.dot(mlp_in, gate_up[:, 0, :], preferred_element_type=jnp.float32)
    up_rows = jnp.dot(mlp_in, gate_up[:, 1, :], preferred_element_type=jnp.float32)
    hidden = (jax.nn.silu(gate_rows) * up_rows).astype(jnp.bfloat16)
    layer_rows = (residual + blockwise_down(hidden, down_weight)).astype(jnp.bfloat16)
    return (layer_rows[:prefill_count], layer_rows[prefill_count:], cache_after)

def reference(prefill_rows, decode_rows, cache_pool, page_table, lengths, destination, attn_gain, inproj_weight, inproj_bias, outproj_weight, mlp_gain, gate_up, down_weight):

    def column(column_args):
        prefill_x, decode_x, pool_rows, table_rows, length_rows, dest_rows = column_args
        n_req = pool_rows.shape[0]
        slot_total = dest_rows.shape[1]
        gathered = jax.vmap(lambda pool_one, table_one: pool_one[table_one].reshape(table_one.shape[0], -1, pool_one.shape[-1]))(pool_rows, table_rows)
        decode_caches = gathered[:, :slot_total]
        contexts = gathered[:, slot_total]
        flat_ids = jnp.arange(n_req * slot_total, dtype=jnp.int32)
        sort_keys = dest_rows.reshape(-1).astype(jnp.int32) * (n_req * slot_total) + flat_ids
        arrival_order = jnp.argsort(sort_keys).astype(jnp.int32)
        moved_cache = decode_caches.reshape((n_req * slot_total,) + decode_caches.shape[2:])[arrival_order].reshape(decode_caches.shape)
        moved_rows = decode_x.reshape(n_req * slot_total, -1)[arrival_order].reshape(decode_x.shape)
        moved_length = length_rows[:, :slot_total].reshape(-1)[arrival_order].reshape(n_req, slot_total)

        def one_device(device_args):
            return device_layer(*device_args, attn_gain, inproj_weight, inproj_bias, outproj_weight, mlp_gain, gate_up, down_weight)
        return lax.map(one_device, (prefill_x, contexts, length_rows[:, slot_total], moved_rows, moved_cache, moved_length))
    return lax.map(column, (prefill_rows, decode_rows, cache_pool, page_table, lengths, destination))
```

```python
import math

import jax
import jax.numpy as jnp
from jax import lax
from jax.sharding import PartitionSpec as P

QUERY_HEADS = 12
KEY_VALUE_HEADS = 2
HEAD_SIZE = 128
CAP = 2


rms_eps = 1e-06
rope_base = 1000000.0


def rms_scale(rows, gain_row):
    rows_wide = rows.astype(jnp.float32)
    inverse = lax.rsqrt(jnp.mean(rows_wide * rows_wide, axis=-1, keepdims=True) + rms_eps)
    return (rows_wide * inverse * gain_row.astype(jnp.float32)).astype(jnp.bfloat16)


def apply_rotary(vectors, token_positions):
    head_dim = vectors.shape[-1]
    half_dim = head_dim // 2
    frequency = rope_base ** (-2.0 * jnp.arange(half_dim, dtype=jnp.float32) / head_dim)
    angles = token_positions.astype(jnp.float32)[:, None] * frequency[None, :]
    cosine = jnp.concatenate([jnp.cos(angles), jnp.cos(angles)], axis=-1)[:, None, :]
    sine_table = jnp.concatenate([jnp.sin(angles), jnp.sin(angles)], axis=-1)[:, None, :]
    turned = jnp.concatenate([-vectors[..., half_dim:], vectors[..., :half_dim]], axis=-1)
    return vectors * cosine + turned * sine_table


def project(normed, weight, bias_row, token_positions):
    mixed_batch = jnp.dot(normed, weight, preferred_element_type=jnp.float32) + bias_row.astype(
        jnp.float32
    )
    query_head_width = QUERY_HEADS * HEAD_SIZE
    key_head_width = KEY_VALUE_HEADS * HEAD_SIZE
    query_rows = apply_rotary(
        mixed_batch[:, :query_head_width].reshape(-1, QUERY_HEADS, HEAD_SIZE), token_positions
    )
    key_row_block = apply_rotary(
        mixed_batch[:, query_head_width : query_head_width + key_head_width].reshape(
            -1, KEY_VALUE_HEADS, HEAD_SIZE
        ),
        token_positions,
    )
    value_rows = mixed_batch[:, query_head_width + key_head_width :]
    key_value_pair = jnp.concatenate(
        [key_row_block.reshape(-1, key_head_width), value_rows], axis=-1
    )
    return (
        query_rows.reshape(-1, query_head_width).astype(jnp.bfloat16),
        key_value_pair.astype(jnp.bfloat16),
    )


def attend(query_rows, key_value_pair, allowed):
    batch_count = query_rows.shape[0]
    total_rows = query_rows.shape[1]
    group_width = QUERY_HEADS // KEY_VALUE_HEADS
    key_head_width = KEY_VALUE_HEADS * HEAD_SIZE
    grouped_heads = query_rows.reshape(
        batch_count, total_rows, KEY_VALUE_HEADS, group_width, HEAD_SIZE
    )
    key_row_block = key_value_pair[:, :, :key_head_width].reshape(
        batch_count, -1, KEY_VALUE_HEADS, HEAD_SIZE
    )
    value_rows = key_value_pair[:, :, key_head_width:].reshape(
        batch_count, -1, KEY_VALUE_HEADS, HEAD_SIZE
    )
    scores = jnp.einsum(
        "bqhgd,bkhd->bhgqk", grouped_heads, key_row_block, preferred_element_type=jnp.float32
    ) / math.sqrt(HEAD_SIZE)
    scores = jnp.where(allowed[:, None, None, :, :], scores, -jnp.inf)
    row_max = jnp.max(scores, axis=-1, keepdims=True)
    weights = jnp.exp(scores - row_max)
    weights = (weights / jnp.sum(weights, axis=-1, keepdims=True)).astype(jnp.bfloat16)
    result = jnp.einsum(
        "bhgqk,bkhd->bqhgd", weights, value_rows, preferred_element_type=jnp.float32
    )
    return result.reshape(batch_count, total_rows, QUERY_HEADS * HEAD_SIZE).astype(jnp.bfloat16)


def extend(cache_rows, key_value_pair, lengths_now):
    token_positions = jnp.arange(cache_rows.shape[1], dtype=jnp.int32)[None, :, None]
    limit = lengths_now[:, None, None]
    return jnp.where(
        token_positions < limit,
        cache_rows,
        jnp.where(token_positions == limit, key_value_pair[:, None, :], jnp.zeros_like(cache_rows)),
    )


def shards(
    prefill_rows,
    decode_rows,
    cache_pool,
    page_table,
    lengths,
    destination,
    attn_gain,
    inproj_weight,
    inproj_bias,
    outproj_weight,
    mlp_gain,
    gate_up,
    down_weight,
):
    n_req = lax.axis_size("req")
    own_index = lax.axis_index("req")
    slot_total = destination.shape[2]
    pool_rows = cache_pool[0, 0]
    table_rows = page_table[0, 0]
    width_per_row = pool_rows.shape[-1]
    cache_length = table_rows.shape[1] * pool_rows.shape[1]
    context = pool_rows[table_rows[slot_total]].reshape(cache_length, width_per_row)
    context_length = lengths[0, 0, slot_total]
    slot_ids = jnp.arange(slot_total, dtype=jnp.int32)

    local_down = jnp.transpose(down_weight)[:, None, :]
    all_weights = lax.all_gather(
        jnp.concatenate([gate_up, local_down], axis=1), "req", axis=0, tiled=True
    )

    send_dest = destination[0, 0]
    decode_x = decode_rows[0, 0]
    own_len = lengths[0, 0, :slot_total]
    same_dest = send_dest[None, :] == send_dest[:, None]
    earlier = same_dest & (slot_ids[None, :] < slot_ids[:, None])
    within = jnp.sum(earlier.astype(jnp.int32), axis=1)
    target = send_dest * CAP + within
    flat_slots = jnp.arange(n_req * CAP, dtype=jnp.int32)
    matches = target[None, :] == flat_slots[:, None]
    picked = jnp.sum(jnp.where(matches, slot_ids[None, :], 0), axis=1)
    send_pages = table_rows[picked]
    send_cache = pool_rows[send_pages].reshape(n_req, CAP, cache_length, width_per_row)
    send_x = decode_x[picked].reshape(n_req, CAP, -1)
    send_len = jnp.broadcast_to(own_len[picked].reshape(n_req, CAP, 1), (n_req, CAP, 128))
    recv_cache = lax.all_to_all(send_cache, "req", split_axis=0, concat_axis=0, tiled=True)
    recv_x = lax.all_to_all(send_x, "req", split_axis=0, concat_axis=0, tiled=True)
    recv_len = lax.all_to_all(send_len, "req", split_axis=0, concat_axis=0, tiled=True)

    shift = jnp.mod(send_dest - own_index, n_req)
    source = jnp.mod(own_index - shift, n_req)
    order_key = source * slot_total + slot_ids
    rank = jnp.sum((order_key[None, :] < order_key[:, None]).astype(jnp.int32), axis=1)
    chosen = rank[None, :] == slot_ids[:, None]
    arrival_order = jnp.sum(jnp.where(chosen, (source * CAP + within)[None, :], 0), axis=1)
    got_cache = recv_cache.reshape(n_req * CAP, cache_length, width_per_row)[arrival_order]
    got_x = recv_x.reshape(n_req * CAP, -1)[arrival_order]
    got_length = recv_len.reshape(n_req * CAP, 128)[arrival_order, 0]

    prefill_x = prefill_rows[0, 0]
    prefill_count = prefill_x.shape[0]
    block_ids = jnp.arange(prefill_count, dtype=jnp.int32)
    cache_ids = jnp.arange(cache_length, dtype=jnp.int32)
    prefill_q, prefill_kv = project(
        rms_scale(prefill_x, attn_gain), inproj_weight, inproj_bias, context_length + block_ids
    )
    key_block = jnp.concatenate([context, prefill_kv], axis=0)
    allowed = jnp.concatenate(
        [
            jnp.broadcast_to(cache_ids[None, :] < context_length, (prefill_count, cache_length)),
            block_ids[None, :] <= block_ids[:, None],
        ],
        axis=1,
    )
    prefill_att = attend(prefill_q[None], key_block[None], allowed[None])[0]
    prefill_res = prefill_x.astype(jnp.float32) + jnp.dot(
        prefill_att, outproj_weight, preferred_element_type=jnp.float32
    )
    prefill_out = feed_forward(prefill_res, mlp_gain, all_weights)

    decode_q, decode_kv = project(
        rms_scale(got_x, attn_gain), inproj_weight, inproj_bias, got_length
    )
    cache_after = extend(got_cache, decode_kv, got_length)
    decode_allowed = (cache_ids[None, :] <= got_length[:, None])[:, None, :]
    decode_att = attend(decode_q[:, None, :], cache_after, decode_allowed)[:, 0]
    decode_res = got_x.astype(jnp.float32) + jnp.dot(
        decode_att, outproj_weight, preferred_element_type=jnp.float32
    )
    decode_out = feed_forward(decode_res, mlp_gain, all_weights)
    return (
        prefill_out[None, None],
        decode_out[None, None],
        cache_after[None, None],
    )


def feed_forward(residual, mlp_gain, all_weights):
    mlp_in = rms_scale(residual, mlp_gain)
    gate_and_up = jnp.einsum(
        "nd,dkf->nkf",
        lax.all_gather(mlp_in, "blk", axis=0, tiled=True),
        all_weights[:, :2, :],
        preferred_element_type=jnp.float32,
    )
    hidden = (jax.nn.silu(gate_and_up[:, 0, :]) * gate_and_up[:, 1, :]).astype(jnp.bfloat16)
    partial = jnp.einsum(
        "nf,df->nd", hidden, all_weights[:, 2, :], preferred_element_type=jnp.float32
    ).astype(jnp.bfloat16)
    mlp_rows = lax.psum_scatter(partial, "blk", scatter_dimension=0, tiled=True)
    return (residual + mlp_rows.astype(jnp.float32)).astype(jnp.bfloat16)


def solution(mesh):
    return jax.shard_map(
        shards,
        mesh=mesh,
        in_specs=(
            P("blk", "req", None, None),
            P("blk", "req", None, None),
            P("blk", "req", None, None, None),
            P("blk", "req", None, None),
            P("blk", "req", None),
            P("blk", "req", None),
            P(),
            P(),
            P(),
            P(),
            P(),
            P("req", None, "blk"),
            P("blk", "req"),
        ),
        out_specs=(
            P("blk", "req", None, None),
            P("blk", "req", None, None),
            P("blk", "req", None, None, None),
        ),
        check_vma=False,
    )
```

```python
import math

import jax
import jax.numpy as jnp
from jax import lax
from jax.sharding import PartitionSpec as P

QUERY_HEADS = 12
KEY_VALUE_HEADS = 2
HEAD_SIZE = 128
CAP = 2


rms_eps = 1e-06
rope_base = 1000000.0


def rms_scale(rows, gain_row):
    rows_wide = rows.astype(jnp.float32)
    inverse = lax.rsqrt(jnp.mean(rows_wide * rows_wide, axis=-1, keepdims=True) + rms_eps)
    return (rows_wide * inverse * gain_row.astype(jnp.float32)).astype(jnp.bfloat16)


def apply_rotary(vectors, token_positions):
    head_dim = vectors.shape[-1]
    half_dim = head_dim // 2
    frequency = rope_base ** (-2.0 * jnp.arange(half_dim, dtype=jnp.float32) / head_dim)
    angles = token_positions.astype(jnp.float32)[:, None] * frequency[None, :]
    cosine = jnp.concatenate([jnp.cos(angles), jnp.cos(angles)], axis=-1)[:, None, :]
    sine_table = jnp.concatenate([jnp.sin(angles), jnp.sin(angles)], axis=-1)[:, None, :]
    turned = jnp.concatenate([-vectors[..., half_dim:], vectors[..., :half_dim]], axis=-1)
    return vectors * cosine + turned * sine_table


def project(normed, weight, bias_row, token_positions):
    mixed_batch = jnp.dot(normed, weight, preferred_element_type=jnp.float32) + bias_row.astype(
        jnp.float32
    )
    query_head_width = QUERY_HEADS * HEAD_SIZE
    key_head_width = KEY_VALUE_HEADS * HEAD_SIZE
    query_rows = apply_rotary(
        mixed_batch[:, :query_head_width].reshape(-1, QUERY_HEADS, HEAD_SIZE), token_positions
    )
    key_row_block = apply_rotary(
        mixed_batch[:, query_head_width : query_head_width + key_head_width].reshape(
            -1, KEY_VALUE_HEADS, HEAD_SIZE
        ),
        token_positions,
    )
    value_rows = mixed_batch[:, query_head_width + key_head_width :]
    key_value_pair = jnp.concatenate(
        [key_row_block.reshape(-1, key_head_width), value_rows], axis=-1
    )
    return (
        query_rows.reshape(-1, query_head_width).astype(jnp.bfloat16),
        key_value_pair.astype(jnp.bfloat16),
    )


def attend(query_rows, key_value_pair, allowed):
    batch_count = query_rows.shape[0]
    total_rows = query_rows.shape[1]
    group_width = QUERY_HEADS // KEY_VALUE_HEADS
    key_head_width = KEY_VALUE_HEADS * HEAD_SIZE
    grouped_heads = query_rows.reshape(
        batch_count, total_rows, KEY_VALUE_HEADS, group_width, HEAD_SIZE
    )
    key_row_block = key_value_pair[:, :, :key_head_width].reshape(
        batch_count, -1, KEY_VALUE_HEADS, HEAD_SIZE
    )
    value_rows = key_value_pair[:, :, key_head_width:].reshape(
        batch_count, -1, KEY_VALUE_HEADS, HEAD_SIZE
    )
    scores = jnp.einsum(
        "bqhgd,bkhd->bhgqk", grouped_heads, key_row_block, preferred_element_type=jnp.float32
    ) / math.sqrt(HEAD_SIZE)
    scores = jnp.where(allowed[:, None, None, :, :], scores, -jnp.inf)
    row_max = jnp.max(scores, axis=-1, keepdims=True)
    weights = jnp.exp(scores - row_max)
    weights = (weights / jnp.sum(weights, axis=-1, keepdims=True)).astype(jnp.bfloat16)
    result = jnp.einsum(
        "bhgqk,bkhd->bqhgd", weights, value_rows, preferred_element_type=jnp.float32
    )
    return result.reshape(batch_count, total_rows, QUERY_HEADS * HEAD_SIZE).astype(jnp.bfloat16)


def extend(cache_rows, key_value_pair, lengths_now):
    token_positions = jnp.arange(cache_rows.shape[1], dtype=jnp.int32)[None, :, None]
    limit = lengths_now[:, None, None]
    return jnp.where(
        token_positions < limit,
        cache_rows,
        jnp.where(token_positions == limit, key_value_pair[:, None, :], jnp.zeros_like(cache_rows)),
    )


def shards(
    prefill_rows,
    decode_rows,
    cache_pool,
    page_table,
    lengths,
    destination,
    attn_gain,
    inproj_weight,
    inproj_bias,
    outproj_weight,
    mlp_gain,
    gate_up,
    down_weight,
):
    n_req = lax.axis_size("req")
    own_index = lax.axis_index("req")
    slot_total = destination.shape[2]
    pool_rows = cache_pool[0, 0]
    table_rows = page_table[0, 0]
    width_per_row = pool_rows.shape[-1]
    cache_length = table_rows.shape[1] * pool_rows.shape[1]
    context = pool_rows[table_rows[slot_total]].reshape(cache_length, width_per_row)
    context_length = lengths[0, 0, slot_total]
    slot_ids = jnp.arange(slot_total, dtype=jnp.int32)

    local_down = jnp.transpose(down_weight)[:, None, :]
    all_weights = lax.all_gather(
        jnp.concatenate([gate_up, local_down], axis=1), "req", axis=0, tiled=True
    )

    send_dest = destination[0, 0]
    decode_x = decode_rows[0, 0]
    own_len = lengths[0, 0, :slot_total]
    same_dest = send_dest[None, :] == send_dest[:, None]
    earlier = same_dest & (slot_ids[None, :] < slot_ids[:, None])
    within = jnp.sum(earlier.astype(jnp.int32), axis=1)
    target = send_dest * CAP + within
    flat_slots = jnp.arange(n_req * CAP, dtype=jnp.int32)
    matches = target[None, :] == flat_slots[:, None]
    picked = jnp.sum(jnp.where(matches, slot_ids[None, :], 0), axis=1)
    send_pages = table_rows[picked]
    send_cache = pool_rows[send_pages].reshape(n_req, CAP, cache_length, width_per_row)
    send_x = decode_x[picked].reshape(n_req, CAP, -1)
    send_len = jnp.broadcast_to(own_len[picked].reshape(n_req, CAP, 1), (n_req, CAP, 128))
    recv_cache = lax.all_to_all(send_cache, "req", split_axis=0, concat_axis=0, tiled=True)
    recv_x = lax.all_to_all(send_x, "req", split_axis=0, concat_axis=0, tiled=True)
    recv_len = lax.all_to_all(send_len, "req", split_axis=0, concat_axis=0, tiled=True)

    shift = jnp.mod(send_dest - own_index, n_req)
    source = jnp.mod(own_index - shift, n_req)
    order_key = source * slot_total + slot_ids
    rank = jnp.sum((order_key[None, :] < order_key[:, None]).astype(jnp.int32), axis=1)
    chosen = rank[None, :] == slot_ids[:, None]
    arrival_order = jnp.sum(jnp.where(chosen, (source * CAP + within)[None, :], 0), axis=1)

    prefill_x = prefill_rows[0, 0]
    prefill_count = prefill_x.shape[0]
    block_ids = jnp.arange(prefill_count, dtype=jnp.int32)
    cache_ids = jnp.arange(cache_length, dtype=jnp.int32)
    prefill_q, prefill_kv = project(
        rms_scale(prefill_x, attn_gain), inproj_weight, inproj_bias, context_length + block_ids
    )
    key_block = jnp.concatenate([context, prefill_kv], axis=0)
    allowed = jnp.concatenate(
        [
            jnp.broadcast_to(cache_ids[None, :] < context_length, (prefill_count, cache_length)),
            block_ids[None, :] <= block_ids[:, None],
        ],
        axis=1,
    )
    prefill_att = attend(prefill_q[None], key_block[None], allowed[None])[0]
    prefill_res = prefill_x.astype(jnp.float32) + jnp.dot(
        prefill_att, outproj_weight, preferred_element_type=jnp.float32
    )
    prefill_partial = feed_forward_partial(prefill_res, mlp_gain, all_weights)
    prefill_out = feed_forward_finish(prefill_res, prefill_partial)
    prefill_out, recv_cache, recv_x, recv_len = lax.optimization_barrier(
        (prefill_out, recv_cache, recv_x, recv_len)
    )
    got_cache = recv_cache.reshape(n_req * CAP, cache_length, width_per_row)[arrival_order]
    got_x = recv_x.reshape(n_req * CAP, -1)[arrival_order]
    got_length = recv_len.reshape(n_req * CAP, 128)[arrival_order, 0]

    decode_q, decode_kv = project(
        rms_scale(got_x, attn_gain), inproj_weight, inproj_bias, got_length
    )
    cache_after = extend(got_cache, decode_kv, got_length)
    decode_allowed = (cache_ids[None, :] <= got_length[:, None])[:, None, :]
    decode_att = attend(decode_q[:, None, :], cache_after, decode_allowed)[:, 0]
    decode_res = got_x.astype(jnp.float32) + jnp.dot(
        decode_att, outproj_weight, preferred_element_type=jnp.float32
    )
    decode_out = feed_forward_finish(
        decode_res, feed_forward_partial(decode_res, mlp_gain, all_weights)
    )
    return (
        prefill_out[None, None],
        decode_out[None, None],
        cache_after[None, None],
    )


def feed_forward_partial(residual, mlp_gain, all_weights):
    mlp_in = rms_scale(residual, mlp_gain)
    gate_and_up = jnp.einsum(
        "nd,dkf->nkf",
        lax.all_gather(mlp_in, "blk", axis=0, tiled=True),
        all_weights[:, :2, :],
        preferred_element_type=jnp.float32,
    )
    hidden = (jax.nn.silu(gate_and_up[:, 0, :]) * gate_and_up[:, 1, :]).astype(jnp.bfloat16)
    return jnp.einsum(
        "nf,df->nd", hidden, all_weights[:, 2, :], preferred_element_type=jnp.float32
    ).astype(jnp.bfloat16)


def feed_forward_finish(residual, partial):
    mlp_rows = lax.psum_scatter(partial, "blk", scatter_dimension=0, tiled=True)
    return (residual + mlp_rows.astype(jnp.float32)).astype(jnp.bfloat16)


def solution(mesh):
    return jax.shard_map(
        shards,
        mesh=mesh,
        in_specs=(
            P("blk", "req", None, None),
            P("blk", "req", None, None),
            P("blk", "req", None, None, None),
            P("blk", "req", None, None),
            P("blk", "req", None),
            P("blk", "req", None),
            P(),
            P(),
            P(),
            P(),
            P(),
            P("req", None, "blk"),
            P("blk", "req"),
        ),
        out_specs=(
            P("blk", "req", None, None),
            P("blk", "req", None, None),
            P("blk", "req", None, None, None),
        ),
        check_vma=False,
    )
```

```python
import math

import jax
import jax.numpy as jnp
from jax import lax
from jax.sharding import PartitionSpec as P

QUERY_HEADS = 12
KEY_VALUE_HEADS = 2
HEAD_SIZE = 128
CAP = 2


rms_eps = 1e-06
rope_base = 1000000.0


def rms_scale(rows, gain_row):
    rows_wide = rows.astype(jnp.float32)
    inverse = lax.rsqrt(jnp.mean(rows_wide * rows_wide, axis=-1, keepdims=True) + rms_eps)
    return (rows_wide * inverse * gain_row.astype(jnp.float32)).astype(jnp.bfloat16)


def apply_rotary(vectors, token_positions):
    head_dim = vectors.shape[-1]
    half_dim = head_dim // 2
    frequency = rope_base ** (-2.0 * jnp.arange(half_dim, dtype=jnp.float32) / head_dim)
    angles = token_positions.astype(jnp.float32)[:, None] * frequency[None, :]
    cosine = jnp.concatenate([jnp.cos(angles), jnp.cos(angles)], axis=-1)[:, None, :]
    sine_table = jnp.concatenate([jnp.sin(angles), jnp.sin(angles)], axis=-1)[:, None, :]
    turned = jnp.concatenate([-vectors[..., half_dim:], vectors[..., :half_dim]], axis=-1)
    return vectors * cosine + turned * sine_table


def project(normed, weight, bias_row, token_positions):
    mixed_batch = jnp.dot(normed, weight, preferred_element_type=jnp.float32) + bias_row.astype(
        jnp.float32
    )
    query_head_width = QUERY_HEADS * HEAD_SIZE
    key_head_width = KEY_VALUE_HEADS * HEAD_SIZE
    query_rows = apply_rotary(
        mixed_batch[:, :query_head_width].reshape(-1, QUERY_HEADS, HEAD_SIZE), token_positions
    )
    key_row_block = apply_rotary(
        mixed_batch[:, query_head_width : query_head_width + key_head_width].reshape(
            -1, KEY_VALUE_HEADS, HEAD_SIZE
        ),
        token_positions,
    )
    value_rows = mixed_batch[:, query_head_width + key_head_width :]
    key_value_pair = jnp.concatenate(
        [key_row_block.reshape(-1, key_head_width), value_rows], axis=-1
    )
    return (
        query_rows.reshape(-1, query_head_width).astype(jnp.bfloat16),
        key_value_pair.astype(jnp.bfloat16),
    )


def attend(query_rows, key_value_pair, allowed):
    batch_count = query_rows.shape[0]
    total_rows = query_rows.shape[1]
    group_width = QUERY_HEADS // KEY_VALUE_HEADS
    key_head_width = KEY_VALUE_HEADS * HEAD_SIZE
    grouped_heads = query_rows.reshape(
        batch_count, total_rows, KEY_VALUE_HEADS, group_width, HEAD_SIZE
    )
    key_row_block = key_value_pair[:, :, :key_head_width].reshape(
        batch_count, -1, KEY_VALUE_HEADS, HEAD_SIZE
    )
    value_rows = key_value_pair[:, :, key_head_width:].reshape(
        batch_count, -1, KEY_VALUE_HEADS, HEAD_SIZE
    )
    scores = jnp.einsum(
        "bqhgd,bkhd->bhgqk", grouped_heads, key_row_block, preferred_element_type=jnp.float32
    ) / math.sqrt(HEAD_SIZE)
    scores = jnp.where(allowed[:, None, None, :, :], scores, -jnp.inf)
    row_max = jnp.max(scores, axis=-1, keepdims=True)
    weights = jnp.exp(scores - row_max)
    weights = (weights / jnp.sum(weights, axis=-1, keepdims=True)).astype(jnp.bfloat16)
    result = jnp.einsum(
        "bhgqk,bkhd->bqhgd", weights, value_rows, preferred_element_type=jnp.float32
    )
    return result.reshape(batch_count, total_rows, QUERY_HEADS * HEAD_SIZE).astype(jnp.bfloat16)


def extend(cache_rows, key_value_pair, lengths_now):
    token_positions = jnp.arange(cache_rows.shape[1], dtype=jnp.int32)[None, :, None]
    limit = lengths_now[:, None, None]
    return jnp.where(
        token_positions < limit,
        cache_rows,
        jnp.where(token_positions == limit, key_value_pair[:, None, :], jnp.zeros_like(cache_rows)),
    )


def shards(
    prefill_rows,
    decode_rows,
    cache_pool,
    page_table,
    lengths,
    destination,
    attn_gain,
    inproj_weight,
    inproj_bias,
    outproj_weight,
    mlp_gain,
    gate_up,
    down_weight,
):
    n_req = lax.axis_size("req")
    own_index = lax.axis_index("req")
    slot_total = destination.shape[2]
    pool_rows = cache_pool[0, 0]
    table_rows = page_table[0, 0]
    width_per_row = pool_rows.shape[-1]
    cache_length = table_rows.shape[1] * pool_rows.shape[1]
    context = pool_rows[table_rows[slot_total]].reshape(cache_length, width_per_row)
    context_length = lengths[0, 0, slot_total]
    slot_ids = jnp.arange(slot_total, dtype=jnp.int32)

    local_down = jnp.transpose(down_weight)[:, None, :]
    all_weights = lax.all_gather(
        jnp.concatenate([gate_up, local_down], axis=1), "req", axis=0, tiled=True
    )

    send_dest = destination[0, 0]
    decode_x = decode_rows[0, 0]
    own_len = lengths[0, 0, :slot_total]
    same_dest = send_dest[None, :] == send_dest[:, None]
    earlier = same_dest & (slot_ids[None, :] < slot_ids[:, None])
    within = jnp.sum(earlier.astype(jnp.int32), axis=1)
    target = send_dest * CAP + within
    flat_slots = jnp.arange(n_req * CAP, dtype=jnp.int32)
    matches = target[None, :] == flat_slots[:, None]
    picked = jnp.sum(jnp.where(matches, slot_ids[None, :], 0), axis=1)
    send_pages = table_rows[picked]
    send_cache = pool_rows[send_pages].reshape(n_req, CAP, cache_length, width_per_row)
    send_x = decode_x[picked].reshape(n_req, CAP, -1)
    send_len = jnp.broadcast_to(own_len[picked].reshape(n_req, CAP, 1), (n_req, CAP, 128))
    recv_cache = lax.all_to_all(send_cache, "req", split_axis=0, concat_axis=0, tiled=True)
    recv_x = lax.all_to_all(send_x, "req", split_axis=0, concat_axis=0, tiled=True)
    recv_len = lax.all_to_all(send_len, "req", split_axis=0, concat_axis=0, tiled=True)

    shift = jnp.mod(send_dest - own_index, n_req)
    source = jnp.mod(own_index - shift, n_req)
    order_key = source * slot_total + slot_ids
    rank = jnp.sum((order_key[None, :] < order_key[:, None]).astype(jnp.int32), axis=1)
    chosen = rank[None, :] == slot_ids[:, None]
    arrival_order = jnp.sum(jnp.where(chosen, (source * CAP + within)[None, :], 0), axis=1)

    prefill_x = prefill_rows[0, 0]
    prefill_count = prefill_x.shape[0]
    block_ids = jnp.arange(prefill_count, dtype=jnp.int32)
    cache_ids = jnp.arange(cache_length, dtype=jnp.int32)
    prefill_q, prefill_kv = project(
        rms_scale(prefill_x, attn_gain), inproj_weight, inproj_bias, context_length + block_ids
    )
    key_block = jnp.concatenate([context, prefill_kv], axis=0)
    allowed = jnp.concatenate(
        [
            jnp.broadcast_to(cache_ids[None, :] < context_length, (prefill_count, cache_length)),
            block_ids[None, :] <= block_ids[:, None],
        ],
        axis=1,
    )
    prefill_att = attend(prefill_q[None], key_block[None], allowed[None])[0]
    prefill_res = prefill_x.astype(jnp.float32) + jnp.dot(
        prefill_att, outproj_weight, preferred_element_type=jnp.float32
    )
    prefill_partial = feed_forward_partial(prefill_res, mlp_gain, all_weights)
    prefill_partial, recv_cache, recv_x, recv_len = lax.optimization_barrier(
        (prefill_partial, recv_cache, recv_x, recv_len)
    )
    prefill_out = feed_forward_finish(prefill_res, prefill_partial)
    got_cache = recv_cache.reshape(n_req * CAP, cache_length, width_per_row)[arrival_order]
    got_x = recv_x.reshape(n_req * CAP, -1)[arrival_order]
    got_length = recv_len.reshape(n_req * CAP, 128)[arrival_order, 0]

    decode_q, decode_kv = project(
        rms_scale(got_x, attn_gain), inproj_weight, inproj_bias, got_length
    )
    cache_after = extend(got_cache, decode_kv, got_length)
    decode_allowed = (cache_ids[None, :] <= got_length[:, None])[:, None, :]
    decode_att = attend(decode_q[:, None, :], cache_after, decode_allowed)[:, 0]
    decode_res = got_x.astype(jnp.float32) + jnp.dot(
        decode_att, outproj_weight, preferred_element_type=jnp.float32
    )
    decode_out = small_feed_forward(decode_res, mlp_gain, all_weights)
    return (
        prefill_out[None, None],
        decode_out[None, None],
        cache_after[None, None],
    )


def feed_forward_partial(residual, mlp_gain, all_weights):
    mlp_in = rms_scale(residual, mlp_gain)
    gate_and_up = jnp.einsum(
        "nd,dkf->nkf",
        lax.all_gather(mlp_in, "blk", axis=0, tiled=True),
        all_weights[:, :2, :],
        preferred_element_type=jnp.float32,
    )
    hidden = (jax.nn.silu(gate_and_up[:, 0, :]) * gate_and_up[:, 1, :]).astype(jnp.bfloat16)
    return jnp.einsum(
        "nf,df->nd", hidden, all_weights[:, 2, :], preferred_element_type=jnp.float32
    ).astype(jnp.bfloat16)


def small_feed_forward(residual, mlp_gain, all_weights):
    n_blk = lax.axis_size("blk")
    rows = residual.shape[0]
    mlp_in = rms_scale(residual, mlp_gain)
    spread = jnp.broadcast_to(mlp_in[None], (n_blk,) + mlp_in.shape)
    gathered = lax.all_to_all(spread, "blk", split_axis=0, concat_axis=0, tiled=True)
    gate_and_up = jnp.einsum(
        "nd,dkf->nkf",
        gathered.reshape(n_blk * rows, -1),
        all_weights[:, :2, :],
        preferred_element_type=jnp.float32,
    )
    hidden = (jax.nn.silu(gate_and_up[:, 0, :]) * gate_and_up[:, 1, :]).astype(jnp.bfloat16)
    partial = jnp.einsum(
        "nf,df->nd", hidden, all_weights[:, 2, :], preferred_element_type=jnp.float32
    ).astype(jnp.bfloat16)
    returned = lax.all_to_all(
        partial.reshape(n_blk, rows, -1), "blk", split_axis=0, concat_axis=0, tiled=True
    )
    mlp_rows = jnp.sum(returned.astype(jnp.float32), axis=0)
    return (residual + mlp_rows).astype(jnp.bfloat16)


def feed_forward_finish(residual, partial):
    mlp_rows = lax.psum_scatter(partial, "blk", scatter_dimension=0, tiled=True)
    return (residual + mlp_rows.astype(jnp.float32)).astype(jnp.bfloat16)


def solution(mesh):
    return jax.shard_map(
        shards,
        mesh=mesh,
        in_specs=(
            P("blk", "req", None, None),
            P("blk", "req", None, None),
            P("blk", "req", None, None, None),
            P("blk", "req", None, None),
            P("blk", "req", None),
            P("blk", "req", None),
            P(),
            P(),
            P(),
            P(),
            P(),
            P("req", None, "blk"),
            P("blk", "req"),
        ),
        out_specs=(
            P("blk", "req", None, None),
            P("blk", "req", None, None),
            P("blk", "req", None, None, None),
        ),
        check_vma=False,
    )
```

```python
import math

import jax
import jax.numpy as jnp
from jax import lax
from jax.sharding import PartitionSpec as P

QUERY_HEADS = 12
KEY_VALUE_HEADS = 2
HEAD_SIZE = 128
CAP = 2


rms_eps = 1e-06
rope_base = 1000000.0


def rms_scale(rows, gain_row):
    rows_wide = rows.astype(jnp.float32)
    inverse = lax.rsqrt(jnp.mean(rows_wide * rows_wide, axis=-1, keepdims=True) + rms_eps)
    return (rows_wide * inverse * gain_row.astype(jnp.float32)).astype(jnp.bfloat16)


def apply_rotary(vectors, token_positions):
    head_dim = vectors.shape[-1]
    half_dim = head_dim // 2
    frequency = rope_base ** (-2.0 * jnp.arange(half_dim, dtype=jnp.float32) / head_dim)
    angles = token_positions.astype(jnp.float32)[:, None] * frequency[None, :]
    cosine = jnp.concatenate([jnp.cos(angles), jnp.cos(angles)], axis=-1)[:, None, :]
    sine_table = jnp.concatenate([jnp.sin(angles), jnp.sin(angles)], axis=-1)[:, None, :]
    turned = jnp.concatenate([-vectors[..., half_dim:], vectors[..., :half_dim]], axis=-1)
    return vectors * cosine + turned * sine_table


def project(normed, weight, bias_row, token_positions):
    mixed_batch = jnp.dot(normed, weight, preferred_element_type=jnp.float32) + bias_row.astype(
        jnp.float32
    )
    query_head_width = QUERY_HEADS * HEAD_SIZE
    key_head_width = KEY_VALUE_HEADS * HEAD_SIZE
    query_rows = apply_rotary(
        mixed_batch[:, :query_head_width].reshape(-1, QUERY_HEADS, HEAD_SIZE), token_positions
    )
    key_row_block = apply_rotary(
        mixed_batch[:, query_head_width : query_head_width + key_head_width].reshape(
            -1, KEY_VALUE_HEADS, HEAD_SIZE
        ),
        token_positions,
    )
    value_rows = mixed_batch[:, query_head_width + key_head_width :]
    key_value_pair = jnp.concatenate(
        [key_row_block.reshape(-1, key_head_width), value_rows], axis=-1
    )
    return (
        query_rows.reshape(-1, query_head_width).astype(jnp.bfloat16),
        key_value_pair.astype(jnp.bfloat16),
    )


def attend(query_rows, key_value_pair, allowed):
    batch_count = query_rows.shape[0]
    total_rows = query_rows.shape[1]
    group_width = QUERY_HEADS // KEY_VALUE_HEADS
    key_head_width = KEY_VALUE_HEADS * HEAD_SIZE
    grouped_heads = query_rows.reshape(
        batch_count, total_rows, KEY_VALUE_HEADS, group_width, HEAD_SIZE
    )
    key_row_block = key_value_pair[:, :, :key_head_width].reshape(
        batch_count, -1, KEY_VALUE_HEADS, HEAD_SIZE
    )
    value_rows = key_value_pair[:, :, key_head_width:].reshape(
        batch_count, -1, KEY_VALUE_HEADS, HEAD_SIZE
    )
    scores = jnp.einsum(
        "bqhgd,bkhd->bhgqk", grouped_heads, key_row_block, preferred_element_type=jnp.float32
    ) / math.sqrt(HEAD_SIZE)
    scores = jnp.where(allowed[:, None, None, :, :], scores, -jnp.inf)
    row_max = jnp.max(scores, axis=-1, keepdims=True)
    weights = jnp.exp(scores - row_max)
    weights = (weights / jnp.sum(weights, axis=-1, keepdims=True)).astype(jnp.bfloat16)
    result = jnp.einsum(
        "bhgqk,bkhd->bqhgd", weights, value_rows, preferred_element_type=jnp.float32
    )
    return result.reshape(batch_count, total_rows, QUERY_HEADS * HEAD_SIZE).astype(jnp.bfloat16)


def extend(cache_rows, key_value_pair, lengths_now):
    token_positions = jnp.arange(cache_rows.shape[1], dtype=jnp.int32)[None, :, None]
    limit = lengths_now[:, None, None]
    return jnp.where(
        token_positions < limit,
        cache_rows,
        jnp.where(token_positions == limit, key_value_pair[:, None, :], jnp.zeros_like(cache_rows)),
    )


def shards(
    prefill_rows,
    decode_rows,
    cache_pool,
    page_table,
    lengths,
    destination,
    attn_gain,
    inproj_weight,
    inproj_bias,
    outproj_weight,
    mlp_gain,
    gate_up,
    down_weight,
):
    n_req = lax.axis_size("req")
    own_index = lax.axis_index("req")
    slot_total = destination.shape[2]
    pool_rows = cache_pool[0, 0]
    table_rows = page_table[0, 0]
    width_per_row = pool_rows.shape[-1]
    cache_length = table_rows.shape[1] * pool_rows.shape[1]
    context = pool_rows[table_rows[slot_total]].reshape(cache_length, width_per_row)
    context_length = lengths[0, 0, slot_total]
    slot_ids = jnp.arange(slot_total, dtype=jnp.int32)

    local_down = jnp.transpose(down_weight)[:, None, :]
    all_weights = lax.all_gather(
        jnp.concatenate([gate_up, local_down], axis=1), "req", axis=0, tiled=True
    )

    send_dest = destination[0, 0]
    decode_x = decode_rows[0, 0]
    own_len = lengths[0, 0, :slot_total]
    same_dest = send_dest[None, :] == send_dest[:, None]
    earlier = same_dest & (slot_ids[None, :] < slot_ids[:, None])
    within = jnp.sum(earlier.astype(jnp.int32), axis=1)
    target = send_dest * CAP + within
    flat_slots = jnp.arange(n_req * CAP, dtype=jnp.int32)
    matches = target[None, :] == flat_slots[:, None]
    picked = jnp.sum(jnp.where(matches, slot_ids[None, :], 0), axis=1)
    send_pages = table_rows[picked]
    send_cache = pool_rows[send_pages].reshape(n_req, CAP, cache_length, width_per_row)
    send_x = decode_x[picked].reshape(n_req, CAP, -1)
    send_len = jnp.broadcast_to(own_len[picked].reshape(n_req, CAP, 1), (n_req, CAP, 128))
    recv_cache = lax.all_to_all(send_cache, "req", split_axis=0, concat_axis=0, tiled=True)
    recv_x = lax.all_to_all(send_x, "req", split_axis=0, concat_axis=0, tiled=True)
    recv_len = lax.all_to_all(send_len, "req", split_axis=0, concat_axis=0, tiled=True)

    shift = jnp.mod(send_dest - own_index, n_req)
    source = jnp.mod(own_index - shift, n_req)
    order_key = source * slot_total + slot_ids
    rank = jnp.sum((order_key[None, :] < order_key[:, None]).astype(jnp.int32), axis=1)
    chosen = rank[None, :] == slot_ids[:, None]
    arrival_order = jnp.sum(jnp.where(chosen, (source * CAP + within)[None, :], 0), axis=1)

    prefill_x = prefill_rows[0, 0]
    prefill_count = prefill_x.shape[0]
    block_ids = jnp.arange(prefill_count, dtype=jnp.int32)
    cache_ids = jnp.arange(cache_length, dtype=jnp.int32)
    prefill_q, prefill_kv = project(
        rms_scale(prefill_x, attn_gain), inproj_weight, inproj_bias, context_length + block_ids
    )
    key_block = jnp.concatenate([context, prefill_kv], axis=0)
    allowed = jnp.concatenate(
        [
            jnp.broadcast_to(cache_ids[None, :] < context_length, (prefill_count, cache_length)),
            block_ids[None, :] <= block_ids[:, None],
        ],
        axis=1,
    )
    prefill_att = attend(prefill_q[None], key_block[None], allowed[None])[0]
    prefill_res = prefill_x.astype(jnp.float32) + jnp.dot(
        prefill_att, outproj_weight, preferred_element_type=jnp.float32
    )
    all_weights, prefill_res = lax.optimization_barrier((all_weights, prefill_res))
    prefill_partial = feed_forward_partial(prefill_res, mlp_gain, all_weights)
    prefill_partial, recv_cache, recv_x, recv_len = lax.optimization_barrier(
        (prefill_partial, recv_cache, recv_x, recv_len)
    )
    prefill_out = feed_forward_finish(prefill_res, prefill_partial)
    got_cache = recv_cache.reshape(n_req * CAP, cache_length, width_per_row)[arrival_order]
    got_x = recv_x.reshape(n_req * CAP, -1)[arrival_order]
    got_length = recv_len.reshape(n_req * CAP, 128)[arrival_order, 0]

    decode_q, decode_kv = project(
        rms_scale(got_x, attn_gain), inproj_weight, inproj_bias, got_length
    )
    cache_after = extend(got_cache, decode_kv, got_length)
    decode_allowed = (cache_ids[None, :] <= got_length[:, None])[:, None, :]
    decode_att = attend(decode_q[:, None, :], cache_after, decode_allowed)[:, 0]
    decode_res = got_x.astype(jnp.float32) + jnp.dot(
        decode_att, outproj_weight, preferred_element_type=jnp.float32
    )
    decode_out = small_feed_forward(decode_res, mlp_gain, all_weights)
    return (
        prefill_out[None, None],
        decode_out[None, None],
        cache_after[None, None],
    )


def feed_forward_partial(residual, mlp_gain, all_weights):
    mlp_in = rms_scale(residual, mlp_gain)
    gate_and_up = jnp.einsum(
        "nd,dkf->nkf",
        lax.all_gather(mlp_in, "blk", axis=0, tiled=True),
        all_weights[:, :2, :],
        preferred_element_type=jnp.float32,
    )
    hidden = (jax.nn.silu(gate_and_up[:, 0, :]) * gate_and_up[:, 1, :]).astype(jnp.bfloat16)
    return jnp.einsum(
        "nf,df->nd", hidden, all_weights[:, 2, :], preferred_element_type=jnp.float32
    ).astype(jnp.bfloat16)


def small_feed_forward(residual, mlp_gain, all_weights):
    n_blk = lax.axis_size("blk")
    rows = residual.shape[0]
    mlp_in = rms_scale(residual, mlp_gain)
    spread = jnp.broadcast_to(mlp_in[None], (n_blk,) + mlp_in.shape)
    gathered = lax.all_to_all(spread, "blk", split_axis=0, concat_axis=0, tiled=True)
    gate_and_up = jnp.einsum(
        "nd,dkf->nkf",
        gathered.reshape(n_blk * rows, -1),
        all_weights[:, :2, :],
        preferred_element_type=jnp.float32,
    )
    hidden = (jax.nn.silu(gate_and_up[:, 0, :]) * gate_and_up[:, 1, :]).astype(jnp.bfloat16)
    partial = jnp.einsum(
        "nf,df->nd", hidden, all_weights[:, 2, :], preferred_element_type=jnp.float32
    ).astype(jnp.bfloat16)
    returned = lax.all_to_all(
        partial.reshape(n_blk, rows, -1), "blk", split_axis=0, concat_axis=0, tiled=True
    )
    mlp_rows = jnp.sum(returned.astype(jnp.float32), axis=0)
    return (residual + mlp_rows).astype(jnp.bfloat16)


def feed_forward_finish(residual, partial):
    mlp_rows = lax.psum_scatter(partial, "blk", scatter_dimension=0, tiled=True)
    return (residual + mlp_rows.astype(jnp.float32)).astype(jnp.bfloat16)


def solution(mesh):
    return jax.shard_map(
        shards,
        mesh=mesh,
        in_specs=(
            P("blk", "req", None, None),
            P("blk", "req", None, None),
            P("blk", "req", None, None, None),
            P("blk", "req", None, None),
            P("blk", "req", None),
            P("blk", "req", None),
            P(),
            P(),
            P(),
            P(),
            P(),
            P("req", None, "blk"),
            P("blk", "req"),
        ),
        out_specs=(
            P("blk", "req", None, None),
            P("blk", "req", None, None),
            P("blk", "req", None, None, None),
        ),
        check_vma=False,
    )
```

```python
import math

import jax
import jax.numpy as jnp
from jax import lax
from jax.sharding import PartitionSpec as P

QUERY_HEADS = 12
KEY_VALUE_HEADS = 2
HEAD_SIZE = 128
CAP = 2


rms_eps = 1e-06
rope_base = 1000000.0


def rms_scale(rows, gain_row):
    rows_wide = rows.astype(jnp.float32)
    inverse = lax.rsqrt(jnp.mean(rows_wide * rows_wide, axis=-1, keepdims=True) + rms_eps)
    return (rows_wide * inverse * gain_row.astype(jnp.float32)).astype(jnp.bfloat16)


def apply_rotary(vectors, token_positions):
    head_dim = vectors.shape[-1]
    half_dim = head_dim // 2
    frequency = rope_base ** (-2.0 * jnp.arange(half_dim, dtype=jnp.float32) / head_dim)
    angles = token_positions.astype(jnp.float32)[:, None] * frequency[None, :]
    cosine = jnp.concatenate([jnp.cos(angles), jnp.cos(angles)], axis=-1)[:, None, :]
    sine_table = jnp.concatenate([jnp.sin(angles), jnp.sin(angles)], axis=-1)[:, None, :]
    turned = jnp.concatenate([-vectors[..., half_dim:], vectors[..., :half_dim]], axis=-1)
    return vectors * cosine + turned * sine_table


def project(normed, weight, bias_row, token_positions):
    mixed_batch = jnp.dot(normed, weight, preferred_element_type=jnp.float32) + bias_row.astype(
        jnp.float32
    )
    query_head_width = QUERY_HEADS * HEAD_SIZE
    key_head_width = KEY_VALUE_HEADS * HEAD_SIZE
    query_rows = apply_rotary(
        mixed_batch[:, :query_head_width].reshape(-1, QUERY_HEADS, HEAD_SIZE), token_positions
    )
    key_row_block = apply_rotary(
        mixed_batch[:, query_head_width : query_head_width + key_head_width].reshape(
            -1, KEY_VALUE_HEADS, HEAD_SIZE
        ),
        token_positions,
    )
    value_rows = mixed_batch[:, query_head_width + key_head_width :]
    key_value_pair = jnp.concatenate(
        [key_row_block.reshape(-1, key_head_width), value_rows], axis=-1
    )
    return (
        query_rows.reshape(-1, query_head_width).astype(jnp.bfloat16),
        key_value_pair.astype(jnp.bfloat16),
    )


def attend(query_rows, key_value_pair, allowed):
    batch_count = query_rows.shape[0]
    total_rows = query_rows.shape[1]
    group_width = QUERY_HEADS // KEY_VALUE_HEADS
    key_head_width = KEY_VALUE_HEADS * HEAD_SIZE
    grouped_heads = query_rows.reshape(
        batch_count, total_rows, KEY_VALUE_HEADS, group_width, HEAD_SIZE
    )
    key_row_block = key_value_pair[:, :, :key_head_width].reshape(
        batch_count, -1, KEY_VALUE_HEADS, HEAD_SIZE
    )
    value_rows = key_value_pair[:, :, key_head_width:].reshape(
        batch_count, -1, KEY_VALUE_HEADS, HEAD_SIZE
    )
    scores = jnp.einsum(
        "bqhgd,bkhd->bhgqk", grouped_heads, key_row_block, preferred_element_type=jnp.float32
    ) / math.sqrt(HEAD_SIZE)
    scores = jnp.where(allowed[:, None, None, :, :], scores, -jnp.inf)
    row_max = jnp.max(scores, axis=-1, keepdims=True)
    weights = jnp.exp(scores - row_max)
    weights = (weights / jnp.sum(weights, axis=-1, keepdims=True)).astype(jnp.bfloat16)
    result = jnp.einsum(
        "bhgqk,bkhd->bqhgd", weights, value_rows, preferred_element_type=jnp.float32
    )
    return result.reshape(batch_count, total_rows, QUERY_HEADS * HEAD_SIZE).astype(jnp.bfloat16)


def extend(cache_rows, key_value_pair, lengths_now):
    token_positions = jnp.arange(cache_rows.shape[1], dtype=jnp.int32)[None, :, None]
    limit = lengths_now[:, None, None]
    return jnp.where(
        token_positions < limit,
        cache_rows,
        jnp.where(token_positions == limit, key_value_pair[:, None, :], jnp.zeros_like(cache_rows)),
    )


def shards(
    prefill_rows,
    decode_rows,
    cache_pool,
    page_table,
    lengths,
    destination,
    attn_gain,
    inproj_weight,
    inproj_bias,
    outproj_weight,
    mlp_gain,
    gate_up,
    down_weight,
):
    n_req = lax.axis_size("req")
    own_index = lax.axis_index("req")
    slot_total = destination.shape[2]
    pool_rows = cache_pool[0, 0]
    table_rows = page_table[0, 0]
    width_per_row = pool_rows.shape[-1]
    cache_length = table_rows.shape[1] * pool_rows.shape[1]
    context = pool_rows[table_rows[slot_total]].reshape(cache_length, width_per_row)
    context_length = lengths[0, 0, slot_total]
    slot_ids = jnp.arange(slot_total, dtype=jnp.int32)

    local_down = jnp.transpose(down_weight)[:, None, :]
    all_weights = lax.all_gather(
        jnp.concatenate([gate_up, local_down], axis=1), "req", axis=0, tiled=True
    )

    send_dest = destination[0, 0]
    decode_x = decode_rows[0, 0]
    own_len = lengths[0, 0, :slot_total]
    same_dest = send_dest[None, :] == send_dest[:, None]
    earlier = same_dest & (slot_ids[None, :] < slot_ids[:, None])
    within = jnp.sum(earlier.astype(jnp.int32), axis=1)
    target = send_dest * CAP + within
    flat_slots = jnp.arange(n_req * CAP, dtype=jnp.int32)
    matches = target[None, :] == flat_slots[:, None]
    picked = jnp.sum(jnp.where(matches, slot_ids[None, :], 0), axis=1)
    send_pages = table_rows[picked]
    send_cache = pool_rows[send_pages].reshape(n_req, CAP, cache_length, width_per_row)
    send_x = decode_x[picked].reshape(n_req, CAP, -1)
    send_len = jnp.broadcast_to(own_len[picked].reshape(n_req, CAP, 1), (n_req, CAP, 128))
    recv_x = lax.all_to_all(send_x, "req", split_axis=0, concat_axis=0, tiled=True)
    recv_len = lax.all_to_all(send_len, "req", split_axis=0, concat_axis=0, tiled=True)

    shift = jnp.mod(send_dest - own_index, n_req)
    source = jnp.mod(own_index - shift, n_req)
    order_key = source * slot_total + slot_ids
    rank = jnp.sum((order_key[None, :] < order_key[:, None]).astype(jnp.int32), axis=1)
    chosen = rank[None, :] == slot_ids[:, None]
    arrival_order = jnp.sum(jnp.where(chosen, (source * CAP + within)[None, :], 0), axis=1)

    prefill_x = prefill_rows[0, 0]
    prefill_count = prefill_x.shape[0]
    block_ids = jnp.arange(prefill_count, dtype=jnp.int32)
    cache_ids = jnp.arange(cache_length, dtype=jnp.int32)
    prefill_q, prefill_kv = project(
        rms_scale(prefill_x, attn_gain), inproj_weight, inproj_bias, context_length + block_ids
    )
    key_block = jnp.concatenate([context, prefill_kv], axis=0)
    allowed = jnp.concatenate(
        [
            jnp.broadcast_to(cache_ids[None, :] < context_length, (prefill_count, cache_length)),
            block_ids[None, :] <= block_ids[:, None],
        ],
        axis=1,
    )
    prefill_att = attend(prefill_q[None], key_block[None], allowed[None])[0]
    prefill_res = prefill_x.astype(jnp.float32) + jnp.dot(
        prefill_att, outproj_weight, preferred_element_type=jnp.float32
    )
    all_weights, prefill_res, send_cache = lax.optimization_barrier(
        (all_weights, prefill_res, send_cache)
    )
    recv_cache = lax.all_to_all(send_cache, "req", split_axis=0, concat_axis=0, tiled=True)
    prefill_partial = feed_forward_partial(prefill_res, mlp_gain, all_weights)
    _, recv_cache, recv_x, recv_len = lax.optimization_barrier(
        (prefill_partial, recv_cache, recv_x, recv_len)
    )
    prefill_out = feed_forward_finish(prefill_res, prefill_partial)
    got_cache = recv_cache.reshape(n_req * CAP, cache_length, width_per_row)[arrival_order]
    got_x = recv_x.reshape(n_req * CAP, -1)[arrival_order]
    got_length = recv_len.reshape(n_req * CAP, 128)[arrival_order, 0]

    decode_q, decode_kv = project(
        rms_scale(got_x, attn_gain), inproj_weight, inproj_bias, got_length
    )
    cache_after = extend(got_cache, decode_kv, got_length)
    decode_allowed = (cache_ids[None, :] <= got_length[:, None])[:, None, :]
    decode_att = attend(decode_q[:, None, :], cache_after, decode_allowed)[:, 0]
    decode_res = got_x.astype(jnp.float32) + jnp.dot(
        decode_att, outproj_weight, preferred_element_type=jnp.float32
    )
    decode_out = small_feed_forward(decode_res, mlp_gain, all_weights)
    return (
        prefill_out[None, None],
        decode_out[None, None],
        cache_after[None, None],
    )


def feed_forward_partial(residual, mlp_gain, all_weights):
    mlp_in = rms_scale(residual, mlp_gain)
    gate_and_up = jnp.einsum(
        "nd,dkf->nkf",
        lax.all_gather(mlp_in, "blk", axis=0, tiled=True),
        all_weights[:, :2, :],
        preferred_element_type=jnp.float32,
    )
    hidden = (jax.nn.silu(gate_and_up[:, 0, :]) * gate_and_up[:, 1, :]).astype(jnp.bfloat16)
    return jnp.einsum(
        "nf,df->nd", hidden, all_weights[:, 2, :], preferred_element_type=jnp.float32
    ).astype(jnp.bfloat16)


def small_feed_forward(residual, mlp_gain, all_weights):
    n_blk = lax.axis_size("blk")
    rows = residual.shape[0]
    mlp_in = rms_scale(residual, mlp_gain)
    spread = jnp.broadcast_to(mlp_in[None], (n_blk,) + mlp_in.shape)
    gathered = lax.all_to_all(spread, "blk", split_axis=0, concat_axis=0, tiled=True)
    gate_and_up = jnp.einsum(
        "nd,dkf->nkf",
        gathered.reshape(n_blk * rows, -1),
        all_weights[:, :2, :],
        preferred_element_type=jnp.float32,
    )
    hidden = (jax.nn.silu(gate_and_up[:, 0, :]) * gate_and_up[:, 1, :]).astype(jnp.bfloat16)
    partial = jnp.einsum(
        "nf,df->nd", hidden, all_weights[:, 2, :], preferred_element_type=jnp.float32
    ).astype(jnp.bfloat16)
    returned = lax.all_to_all(
        partial.reshape(n_blk, rows, -1), "blk", split_axis=0, concat_axis=0, tiled=True
    )
    mlp_rows = jnp.sum(returned.astype(jnp.float32), axis=0)
    return (residual + mlp_rows).astype(jnp.bfloat16)


def feed_forward_finish(residual, partial):
    mlp_rows = lax.psum_scatter(partial, "blk", scatter_dimension=0, tiled=True)
    return (residual + mlp_rows.astype(jnp.float32)).astype(jnp.bfloat16)


def solution(mesh):
    return jax.shard_map(
        shards,
        mesh=mesh,
        in_specs=(
            P("blk", "req", None, None),
            P("blk", "req", None, None),
            P("blk", "req", None, None, None),
            P("blk", "req", None, None),
            P("blk", "req", None),
            P("blk", "req", None),
            P(),
            P(),
            P(),
            P(),
            P(),
            P("req", None, "blk"),
            P("blk", "req"),
        ),
        out_specs=(
            P("blk", "req", None, None),
            P("blk", "req", None, None),
            P("blk", "req", None, None, None),
        ),
        check_vma=False,
    )
```

```python
import math

import jax
import jax.numpy as jnp
from jax import lax
from jax.experimental import pallas as pl
from jax.experimental.pallas import tpu as pltpu
from jax.sharding import PartitionSpec as P

QUERY_HEADS = 12
KEY_VALUE_HEADS = 2
HEAD_SIZE = 128
CAP = 2


rms_eps = 1e-06
rope_base = 1000000.0


def rms_scale(rows, gain_row):
    rows_wide = rows.astype(jnp.float32)
    inverse = lax.rsqrt(jnp.mean(rows_wide * rows_wide, axis=-1, keepdims=True) + rms_eps)
    return (rows_wide * inverse * gain_row.astype(jnp.float32)).astype(jnp.bfloat16)


def apply_rotary(vectors, token_positions):
    head_dim = vectors.shape[-1]
    half_dim = head_dim // 2
    frequency = rope_base ** (-2.0 * jnp.arange(half_dim, dtype=jnp.float32) / head_dim)
    angles = token_positions.astype(jnp.float32)[:, None] * frequency[None, :]
    cosine = jnp.concatenate([jnp.cos(angles), jnp.cos(angles)], axis=-1)[:, None, :]
    sine_table = jnp.concatenate([jnp.sin(angles), jnp.sin(angles)], axis=-1)[:, None, :]
    turned = jnp.concatenate([-vectors[..., half_dim:], vectors[..., :half_dim]], axis=-1)
    return vectors * cosine + turned * sine_table


def project(normed, weight, bias_row, token_positions):
    mixed_batch = jnp.dot(normed, weight, preferred_element_type=jnp.float32) + bias_row.astype(
        jnp.float32
    )
    query_head_width = QUERY_HEADS * HEAD_SIZE
    key_head_width = KEY_VALUE_HEADS * HEAD_SIZE
    query_rows = apply_rotary(
        mixed_batch[:, :query_head_width].reshape(-1, QUERY_HEADS, HEAD_SIZE), token_positions
    )
    key_row_block = apply_rotary(
        mixed_batch[:, query_head_width : query_head_width + key_head_width].reshape(
            -1, KEY_VALUE_HEADS, HEAD_SIZE
        ),
        token_positions,
    )
    value_rows = mixed_batch[:, query_head_width + key_head_width :]
    key_value_pair = jnp.concatenate(
        [key_row_block.reshape(-1, key_head_width), value_rows], axis=-1
    )
    return (
        query_rows.reshape(-1, query_head_width).astype(jnp.bfloat16),
        key_value_pair.astype(jnp.bfloat16),
    )


def attend(query_rows, key_value_pair, allowed):
    batch_count = query_rows.shape[0]
    total_rows = query_rows.shape[1]
    group_width = QUERY_HEADS // KEY_VALUE_HEADS
    key_head_width = KEY_VALUE_HEADS * HEAD_SIZE
    grouped_heads = query_rows.reshape(
        batch_count, total_rows, KEY_VALUE_HEADS, group_width, HEAD_SIZE
    )
    key_row_block = key_value_pair[:, :, :key_head_width].reshape(
        batch_count, -1, KEY_VALUE_HEADS, HEAD_SIZE
    )
    value_rows = key_value_pair[:, :, key_head_width:].reshape(
        batch_count, -1, KEY_VALUE_HEADS, HEAD_SIZE
    )
    scores = jnp.einsum(
        "bqhgd,bkhd->bhgqk", grouped_heads, key_row_block, preferred_element_type=jnp.float32
    ) / math.sqrt(HEAD_SIZE)
    scores = jnp.where(allowed[:, None, None, :, :], scores, -jnp.inf)
    row_max = jnp.max(scores, axis=-1, keepdims=True)
    weights = jnp.exp(scores - row_max)
    weights = (weights / jnp.sum(weights, axis=-1, keepdims=True)).astype(jnp.bfloat16)
    result = jnp.einsum(
        "bhgqk,bkhd->bqhgd", weights, value_rows, preferred_element_type=jnp.float32
    )
    return result.reshape(batch_count, total_rows, QUERY_HEADS * HEAD_SIZE).astype(jnp.bfloat16)


def decode_kernel(order_ref, length_ref, cache_ref, kv_ref, q_ref, new_ref, att_ref):
    limit = length_ref[pl.program_id(0)]
    rows = cache_ref[...]
    positions = lax.broadcasted_iota(jnp.int32, rows.shape, 0)
    extended = jnp.where(
        positions < limit,
        rows,
        jnp.where(positions == limit, kv_ref[...], jnp.zeros_like(rows)),
    )
    new_ref[...] = extended
    group_width = QUERY_HEADS // KEY_VALUE_HEADS
    key_head_width = KEY_VALUE_HEADS * HEAD_SIZE
    key_ids = lax.broadcasted_iota(jnp.int32, (group_width, rows.shape[0]), 1)
    for head in range(KEY_VALUE_HEADS):
        keys = extended[:, head * HEAD_SIZE : (head + 1) * HEAD_SIZE]
        values = extended[:, key_head_width + head * HEAD_SIZE : key_head_width + (head + 1) * HEAD_SIZE]
        scores = lax.dot_general(
            q_ref[head], keys, (((1,), (1,)), ((), ())), preferred_element_type=jnp.float32
        ) / math.sqrt(HEAD_SIZE)
        scores = jnp.where(key_ids <= limit, scores, -jnp.inf)
        weights = jnp.exp(scores - jnp.max(scores, axis=1, keepdims=True))
        weights = (weights / jnp.sum(weights, axis=1, keepdims=True)).astype(jnp.bfloat16)
        att_ref[head] = jnp.dot(weights, values, preferred_element_type=jnp.float32).astype(
            jnp.bfloat16
        )


def decode_attend(arrival_order, got_length, recv_cache, decode_kv, decode_q):
    count = arrival_order.shape[0]
    cache_length, width_per_row = recv_cache.shape[1:]
    group_width = QUERY_HEADS // KEY_VALUE_HEADS
    order = jnp.clip(arrival_order, 0, recv_cache.shape[0] - 1)
    new_cache, attended = pl.pallas_call(
        decode_kernel,
        grid_spec=pltpu.PrefetchScalarGridSpec(
            num_scalar_prefetch=2,
            grid=(count,),
            in_specs=[
                pl.BlockSpec((None, cache_length, width_per_row), lambda p, o, n: (o[p], 0, 0)),
                pl.BlockSpec((None, 1, width_per_row), lambda p, o, n: (p, 0, 0)),
                pl.BlockSpec(
                    (None, KEY_VALUE_HEADS, group_width, HEAD_SIZE), lambda p, o, n: (p, 0, 0, 0)
                ),
            ],
            out_specs=[
                pl.BlockSpec((None, cache_length, width_per_row), lambda p, o, n: (p, 0, 0)),
                pl.BlockSpec(
                    (None, KEY_VALUE_HEADS, group_width, HEAD_SIZE), lambda p, o, n: (p, 0, 0, 0)
                ),
            ],
        ),
        out_shape=[
            jax.ShapeDtypeStruct((count, cache_length, width_per_row), jnp.bfloat16),
            jax.ShapeDtypeStruct((count, KEY_VALUE_HEADS, group_width, HEAD_SIZE), jnp.bfloat16),
        ],
    )(
        order,
        got_length,
        recv_cache,
        decode_kv.reshape(count, 1, width_per_row),
        decode_q.reshape(count, KEY_VALUE_HEADS, group_width, HEAD_SIZE),
    )
    return new_cache, attended.reshape(count, QUERY_HEADS * HEAD_SIZE)


def extend(cache_rows, key_value_pair, lengths_now):
    token_positions = jnp.arange(cache_rows.shape[1], dtype=jnp.int32)[None, :, None]
    limit = lengths_now[:, None, None]
    return jnp.where(
        token_positions < limit,
        cache_rows,
        jnp.where(token_positions == limit, key_value_pair[:, None, :], jnp.zeros_like(cache_rows)),
    )


def shards(
    prefill_rows,
    decode_rows,
    cache_pool,
    page_table,
    lengths,
    destination,
    attn_gain,
    inproj_weight,
    inproj_bias,
    outproj_weight,
    mlp_gain,
    gate_up,
    down_weight,
):
    n_req = lax.axis_size("req")
    own_index = lax.axis_index("req")
    slot_total = destination.shape[2]
    pool_rows = cache_pool[0, 0]
    table_rows = page_table[0, 0]
    width_per_row = pool_rows.shape[-1]
    cache_length = table_rows.shape[1] * pool_rows.shape[1]
    context = pool_rows[table_rows[slot_total]].reshape(cache_length, width_per_row)
    context_length = lengths[0, 0, slot_total]
    slot_ids = jnp.arange(slot_total, dtype=jnp.int32)

    local_down = jnp.transpose(down_weight)[:, None, :]
    all_weights = lax.all_gather(
        jnp.concatenate([gate_up, local_down], axis=1), "req", axis=0, tiled=True
    )

    send_dest = destination[0, 0]
    decode_x = decode_rows[0, 0]
    own_len = lengths[0, 0, :slot_total]
    same_dest = send_dest[None, :] == send_dest[:, None]
    earlier = same_dest & (slot_ids[None, :] < slot_ids[:, None])
    within = jnp.sum(earlier.astype(jnp.int32), axis=1)
    target = send_dest * CAP + within
    flat_slots = jnp.arange(n_req * CAP, dtype=jnp.int32)
    matches = target[None, :] == flat_slots[:, None]
    picked = jnp.sum(jnp.where(matches, slot_ids[None, :], 0), axis=1)
    send_pages = table_rows[picked]
    send_cache = pool_rows[send_pages].reshape(n_req, CAP, cache_length, width_per_row)
    send_x = decode_x[picked].reshape(n_req, CAP, -1)
    send_len = jnp.broadcast_to(own_len[picked].reshape(n_req, CAP, 1), (n_req, CAP, 128))
    recv_x = lax.all_to_all(send_x, "req", split_axis=0, concat_axis=0, tiled=True)
    recv_len = lax.all_to_all(send_len, "req", split_axis=0, concat_axis=0, tiled=True)

    shift = jnp.mod(send_dest - own_index, n_req)
    source = jnp.mod(own_index - shift, n_req)
    order_key = source * slot_total + slot_ids
    rank = jnp.sum((order_key[None, :] < order_key[:, None]).astype(jnp.int32), axis=1)
    chosen = rank[None, :] == slot_ids[:, None]
    arrival_order = jnp.sum(jnp.where(chosen, (source * CAP + within)[None, :], 0), axis=1)

    prefill_x = prefill_rows[0, 0]
    prefill_count = prefill_x.shape[0]
    block_ids = jnp.arange(prefill_count, dtype=jnp.int32)
    cache_ids = jnp.arange(cache_length, dtype=jnp.int32)
    prefill_q, prefill_kv = project(
        rms_scale(prefill_x, attn_gain), inproj_weight, inproj_bias, context_length + block_ids
    )
    key_block = jnp.concatenate([context, prefill_kv], axis=0)
    allowed = jnp.concatenate(
        [
            jnp.broadcast_to(cache_ids[None, :] < context_length, (prefill_count, cache_length)),
            block_ids[None, :] <= block_ids[:, None],
        ],
        axis=1,
    )
    prefill_att = attend(prefill_q[None], key_block[None], allowed[None])[0]
    prefill_res = prefill_x.astype(jnp.float32) + jnp.dot(
        prefill_att, outproj_weight, preferred_element_type=jnp.float32
    )
    all_weights, prefill_res, send_cache = lax.optimization_barrier(
        (all_weights, prefill_res, send_cache)
    )
    recv_cache = lax.all_to_all(send_cache, "req", split_axis=0, concat_axis=0, tiled=True)
    prefill_partial = feed_forward_partial(prefill_res, mlp_gain, all_weights)
    _, recv_cache, recv_x, recv_len = lax.optimization_barrier(
        (prefill_partial, recv_cache, recv_x, recv_len)
    )
    prefill_out = feed_forward_finish(prefill_res, prefill_partial)
    got_x = recv_x.reshape(n_req * CAP, -1)[arrival_order]
    got_length = recv_len.reshape(n_req * CAP, 128)[arrival_order, 0]

    decode_q, decode_kv = project(
        rms_scale(got_x, attn_gain), inproj_weight, inproj_bias, got_length
    )
    cache_after, decode_att = decode_attend(
        arrival_order,
        got_length,
        recv_cache.reshape(n_req * CAP, cache_length, width_per_row),
        decode_kv,
        decode_q,
    )
    decode_res = got_x.astype(jnp.float32) + jnp.dot(
        decode_att, outproj_weight, preferred_element_type=jnp.float32
    )
    decode_out = small_feed_forward(decode_res, mlp_gain, all_weights)
    return (
        prefill_out[None, None],
        decode_out[None, None],
        cache_after[None, None],
    )


def feed_forward_partial(residual, mlp_gain, all_weights):
    mlp_in = rms_scale(residual, mlp_gain)
    gate_and_up = jnp.einsum(
        "nd,dkf->nkf",
        lax.all_gather(mlp_in, "blk", axis=0, tiled=True),
        all_weights[:, :2, :],
        preferred_element_type=jnp.float32,
    )
    hidden = (jax.nn.silu(gate_and_up[:, 0, :]) * gate_and_up[:, 1, :]).astype(jnp.bfloat16)
    return jnp.einsum(
        "nf,df->nd", hidden, all_weights[:, 2, :], preferred_element_type=jnp.float32
    ).astype(jnp.bfloat16)


def small_feed_forward(residual, mlp_gain, all_weights):
    n_blk = lax.axis_size("blk")
    rows = residual.shape[0]
    mlp_in = rms_scale(residual, mlp_gain)
    spread = jnp.broadcast_to(mlp_in[None], (n_blk,) + mlp_in.shape)
    gathered = lax.all_to_all(spread, "blk", split_axis=0, concat_axis=0, tiled=True)
    gate_and_up = jnp.einsum(
        "nd,dkf->nkf",
        gathered.reshape(n_blk * rows, -1),
        all_weights[:, :2, :],
        preferred_element_type=jnp.float32,
    )
    hidden = (jax.nn.silu(gate_and_up[:, 0, :]) * gate_and_up[:, 1, :]).astype(jnp.bfloat16)
    partial = jnp.einsum(
        "nf,df->nd", hidden, all_weights[:, 2, :], preferred_element_type=jnp.float32
    ).astype(jnp.bfloat16)
    returned = lax.all_to_all(
        partial.reshape(n_blk, rows, -1), "blk", split_axis=0, concat_axis=0, tiled=True
    )
    mlp_rows = jnp.sum(returned.astype(jnp.float32), axis=0)
    return (residual + mlp_rows).astype(jnp.bfloat16)


def feed_forward_finish(residual, partial):
    mlp_rows = lax.psum_scatter(partial, "blk", scatter_dimension=0, tiled=True)
    return (residual + mlp_rows.astype(jnp.float32)).astype(jnp.bfloat16)


def solution(mesh):
    return jax.shard_map(
        shards,
        mesh=mesh,
        in_specs=(
            P("blk", "req", None, None),
            P("blk", "req", None, None),
            P("blk", "req", None, None, None),
            P("blk", "req", None, None),
            P("blk", "req", None),
            P("blk", "req", None),
            P(),
            P(),
            P(),
            P(),
            P(),
            P("req", None, "blk"),
            P("blk", "req"),
        ),
        out_specs=(
            P("blk", "req", None, None),
            P("blk", "req", None, None),
            P("blk", "req", None, None, None),
        ),
        check_vma=False,
    )
```

```python
import math

import jax
import jax.numpy as jnp
from jax import lax
from jax.experimental import pallas as pl
from jax.experimental.pallas import tpu as pltpu
from jax.sharding import PartitionSpec as P

QUERY_HEADS = 12
KEY_VALUE_HEADS = 2
HEAD_SIZE = 128
CAP = 2
REQ = ("zx", "core")


rms_eps = 1e-06
rope_base = 1000000.0


def rms_scale(rows, gain_row):
    rows_wide = rows.astype(jnp.float32)
    inverse = lax.rsqrt(jnp.mean(rows_wide * rows_wide, axis=-1, keepdims=True) + rms_eps)
    return (rows_wide * inverse * gain_row.astype(jnp.float32)).astype(jnp.bfloat16)


def apply_rotary(vectors, token_positions):
    head_dim = vectors.shape[-1]
    half_dim = head_dim // 2
    frequency = rope_base ** (-2.0 * jnp.arange(half_dim, dtype=jnp.float32) / head_dim)
    angles = token_positions.astype(jnp.float32)[:, None] * frequency[None, :]
    cosine = jnp.concatenate([jnp.cos(angles), jnp.cos(angles)], axis=-1)[:, None, :]
    sine_table = jnp.concatenate([jnp.sin(angles), jnp.sin(angles)], axis=-1)[:, None, :]
    turned = jnp.concatenate([-vectors[..., half_dim:], vectors[..., :half_dim]], axis=-1)
    return vectors * cosine + turned * sine_table


def project(normed, weight, bias_row, token_positions):
    mixed_batch = jnp.dot(normed, weight, preferred_element_type=jnp.float32) + bias_row.astype(
        jnp.float32
    )
    query_head_width = QUERY_HEADS * HEAD_SIZE
    key_head_width = KEY_VALUE_HEADS * HEAD_SIZE
    query_rows = apply_rotary(
        mixed_batch[:, :query_head_width].reshape(-1, QUERY_HEADS, HEAD_SIZE), token_positions
    )
    key_row_block = apply_rotary(
        mixed_batch[:, query_head_width : query_head_width + key_head_width].reshape(
            -1, KEY_VALUE_HEADS, HEAD_SIZE
        ),
        token_positions,
    )
    value_rows = mixed_batch[:, query_head_width + key_head_width :]
    key_value_pair = jnp.concatenate(
        [key_row_block.reshape(-1, key_head_width), value_rows], axis=-1
    )
    return (
        query_rows.reshape(-1, query_head_width).astype(jnp.bfloat16),
        key_value_pair.astype(jnp.bfloat16),
    )


def attend(query_rows, key_value_pair, allowed):
    batch_count = query_rows.shape[0]
    total_rows = query_rows.shape[1]
    group_width = QUERY_HEADS // KEY_VALUE_HEADS
    key_head_width = KEY_VALUE_HEADS * HEAD_SIZE
    grouped_heads = query_rows.reshape(
        batch_count, total_rows, KEY_VALUE_HEADS, group_width, HEAD_SIZE
    )
    key_row_block = key_value_pair[:, :, :key_head_width].reshape(
        batch_count, -1, KEY_VALUE_HEADS, HEAD_SIZE
    )
    value_rows = key_value_pair[:, :, key_head_width:].reshape(
        batch_count, -1, KEY_VALUE_HEADS, HEAD_SIZE
    )
    scores = jnp.einsum(
        "bqhgd,bkhd->bhgqk", grouped_heads, key_row_block, preferred_element_type=jnp.float32
    ) / math.sqrt(HEAD_SIZE)
    scores = jnp.where(allowed[:, None, None, :, :], scores, -jnp.inf)
    row_max = jnp.max(scores, axis=-1, keepdims=True)
    weights = jnp.exp(scores - row_max)
    weights = (weights / jnp.sum(weights, axis=-1, keepdims=True)).astype(jnp.bfloat16)
    result = jnp.einsum(
        "bhgqk,bkhd->bqhgd", weights, value_rows, preferred_element_type=jnp.float32
    )
    return result.reshape(batch_count, total_rows, QUERY_HEADS * HEAD_SIZE).astype(jnp.bfloat16)


def decode_kernel(order_ref, length_ref, cache_ref, kv_ref, q_ref, new_ref, att_ref):
    limit = length_ref[pl.program_id(0)]
    rows = cache_ref[...]
    positions = lax.broadcasted_iota(jnp.int32, rows.shape, 0)
    extended = jnp.where(
        positions < limit,
        rows,
        jnp.where(positions == limit, kv_ref[...], jnp.zeros_like(rows)),
    )
    new_ref[...] = extended
    group_width = QUERY_HEADS // KEY_VALUE_HEADS
    key_head_width = KEY_VALUE_HEADS * HEAD_SIZE
    key_ids = lax.broadcasted_iota(jnp.int32, (group_width, rows.shape[0]), 1)
    for head in range(KEY_VALUE_HEADS):
        keys = extended[:, head * HEAD_SIZE : (head + 1) * HEAD_SIZE]
        values = extended[:, key_head_width + head * HEAD_SIZE : key_head_width + (head + 1) * HEAD_SIZE]
        scores = lax.dot_general(
            q_ref[head], keys, (((1,), (1,)), ((), ())), preferred_element_type=jnp.float32
        ) / math.sqrt(HEAD_SIZE)
        scores = jnp.where(key_ids <= limit, scores, -jnp.inf)
        weights = jnp.exp(scores - jnp.max(scores, axis=1, keepdims=True))
        weights = (weights / jnp.sum(weights, axis=1, keepdims=True)).astype(jnp.bfloat16)
        att_ref[head] = jnp.dot(weights, values, preferred_element_type=jnp.float32).astype(
            jnp.bfloat16
        )


def decode_attend(arrival_order, got_length, recv_cache, decode_kv, decode_q):
    count = arrival_order.shape[0]
    cache_length, width_per_row = recv_cache.shape[1:]
    group_width = QUERY_HEADS // KEY_VALUE_HEADS
    order = jnp.clip(arrival_order, 0, recv_cache.shape[0] - 1)
    new_cache, attended = pl.pallas_call(
        decode_kernel,
        grid_spec=pltpu.PrefetchScalarGridSpec(
            num_scalar_prefetch=2,
            grid=(count,),
            in_specs=[
                pl.BlockSpec((None, cache_length, width_per_row), lambda p, o, n: (o[p], 0, 0)),
                pl.BlockSpec((None, 1, width_per_row), lambda p, o, n: (p, 0, 0)),
                pl.BlockSpec(
                    (None, KEY_VALUE_HEADS, group_width, HEAD_SIZE), lambda p, o, n: (p, 0, 0, 0)
                ),
            ],
            out_specs=[
                pl.BlockSpec((None, cache_length, width_per_row), lambda p, o, n: (p, 0, 0)),
                pl.BlockSpec(
                    (None, KEY_VALUE_HEADS, group_width, HEAD_SIZE), lambda p, o, n: (p, 0, 0, 0)
                ),
            ],
        ),
        out_shape=[
            jax.ShapeDtypeStruct((count, cache_length, width_per_row), jnp.bfloat16),
            jax.ShapeDtypeStruct((count, KEY_VALUE_HEADS, group_width, HEAD_SIZE), jnp.bfloat16),
        ],
    )(
        order,
        got_length,
        recv_cache,
        decode_kv.reshape(count, 1, width_per_row),
        decode_q.reshape(count, KEY_VALUE_HEADS, group_width, HEAD_SIZE),
    )
    return new_cache, attended.reshape(count, QUERY_HEADS * HEAD_SIZE)


def extend(cache_rows, key_value_pair, lengths_now):
    token_positions = jnp.arange(cache_rows.shape[1], dtype=jnp.int32)[None, :, None]
    limit = lengths_now[:, None, None]
    return jnp.where(
        token_positions < limit,
        cache_rows,
        jnp.where(token_positions == limit, key_value_pair[:, None, :], jnp.zeros_like(cache_rows)),
    )


def shards(
    prefill_rows,
    decode_rows,
    cache_pool,
    page_table,
    lengths,
    destination,
    attn_gain,
    inproj_weight,
    inproj_bias,
    outproj_weight,
    mlp_gain,
    gate_up,
    down_weight,
):
    n_req = lax.axis_size(REQ)
    own_index = lax.axis_index(REQ)
    slot_total = destination.shape[2]
    pool_rows = cache_pool[0, 0]
    table_rows = page_table[0, 0]
    width_per_row = pool_rows.shape[-1]
    cache_length = table_rows.shape[1] * pool_rows.shape[1]
    context = pool_rows[table_rows[slot_total]].reshape(cache_length, width_per_row)
    context_length = lengths[0, 0, slot_total]
    slot_ids = jnp.arange(slot_total, dtype=jnp.int32)

    local_down = jnp.transpose(down_weight)[:, None, :]
    chip_weights = lax.all_gather(jnp.concatenate([gate_up, local_down], axis=1), "zx", axis=0)
    all_weights = lax.all_gather(chip_weights, "core", axis=1)
    all_weights = all_weights.reshape((-1,) + all_weights.shape[3:])

    send_dest = destination[0, 0]
    decode_x = decode_rows[0, 0]
    own_len = lengths[0, 0, :slot_total]
    same_dest = send_dest[None, :] == send_dest[:, None]
    earlier = same_dest & (slot_ids[None, :] < slot_ids[:, None])
    within = jnp.sum(earlier.astype(jnp.int32), axis=1)
    target = send_dest * CAP + within
    flat_slots = jnp.arange(n_req * CAP, dtype=jnp.int32)
    matches = target[None, :] == flat_slots[:, None]
    picked = jnp.sum(jnp.where(matches, slot_ids[None, :], 0), axis=1)
    send_pages = table_rows[picked]
    send_cache = pool_rows[send_pages].reshape(n_req, CAP, cache_length, width_per_row)
    send_x = decode_x[picked].reshape(n_req, CAP, -1)
    send_len = jnp.broadcast_to(own_len[picked].reshape(n_req, CAP, 1), (n_req, CAP, 128))
    recv_x = lax.all_to_all(send_x, REQ, split_axis=0, concat_axis=0, tiled=True)
    recv_len = lax.all_to_all(send_len, REQ, split_axis=0, concat_axis=0, tiled=True)

    shift = jnp.mod(send_dest - own_index, n_req)
    source = jnp.mod(own_index - shift, n_req)
    order_key = source * slot_total + slot_ids
    rank = jnp.sum((order_key[None, :] < order_key[:, None]).astype(jnp.int32), axis=1)
    chosen = rank[None, :] == slot_ids[:, None]
    arrival_order = jnp.sum(jnp.where(chosen, (source * CAP + within)[None, :], 0), axis=1)

    prefill_x = prefill_rows[0, 0]
    prefill_count = prefill_x.shape[0]
    block_ids = jnp.arange(prefill_count, dtype=jnp.int32)
    cache_ids = jnp.arange(cache_length, dtype=jnp.int32)
    prefill_q, prefill_kv = project(
        rms_scale(prefill_x, attn_gain), inproj_weight, inproj_bias, context_length + block_ids
    )
    key_block = jnp.concatenate([context, prefill_kv], axis=0)
    allowed = jnp.concatenate(
        [
            jnp.broadcast_to(cache_ids[None, :] < context_length, (prefill_count, cache_length)),
            block_ids[None, :] <= block_ids[:, None],
        ],
        axis=1,
    )
    prefill_att = attend(prefill_q[None], key_block[None], allowed[None])[0]
    prefill_res = prefill_x.astype(jnp.float32) + jnp.dot(
        prefill_att, outproj_weight, preferred_element_type=jnp.float32
    )
    all_weights, prefill_res, send_cache = lax.optimization_barrier(
        (all_weights, prefill_res, send_cache)
    )
    recv_cache = lax.all_to_all(send_cache, REQ, split_axis=0, concat_axis=0, tiled=True)
    prefill_partial = feed_forward_partial(prefill_res, mlp_gain, all_weights)
    _, recv_cache, recv_x, recv_len = lax.optimization_barrier(
        (prefill_partial, recv_cache, recv_x, recv_len)
    )
    prefill_out = feed_forward_finish(prefill_res, prefill_partial)
    got_x = recv_x.reshape(n_req * CAP, -1)[arrival_order]
    got_length = recv_len.reshape(n_req * CAP, 128)[arrival_order, 0]

    decode_q, decode_kv = project(
        rms_scale(got_x, attn_gain), inproj_weight, inproj_bias, got_length
    )
    cache_after, decode_att = decode_attend(
        arrival_order,
        got_length,
        recv_cache.reshape(n_req * CAP, cache_length, width_per_row),
        decode_kv,
        decode_q,
    )
    decode_res = got_x.astype(jnp.float32) + jnp.dot(
        decode_att, outproj_weight, preferred_element_type=jnp.float32
    )
    decode_out = small_feed_forward(decode_res, mlp_gain, all_weights)
    return (
        prefill_out[None, None],
        decode_out[None, None],
        cache_after[None, None],
    )


def feed_forward_partial(residual, mlp_gain, all_weights):
    mlp_in = rms_scale(residual, mlp_gain)
    gate_and_up = jnp.einsum(
        "nd,dkf->nkf",
        lax.all_gather(mlp_in, "blk", axis=0, tiled=True),
        all_weights[:, :2, :],
        preferred_element_type=jnp.float32,
    )
    hidden = (jax.nn.silu(gate_and_up[:, 0, :]) * gate_and_up[:, 1, :]).astype(jnp.bfloat16)
    return jnp.einsum(
        "nf,df->nd", hidden, all_weights[:, 2, :], preferred_element_type=jnp.float32
    ).astype(jnp.bfloat16)


def small_feed_forward(residual, mlp_gain, all_weights):
    n_blk = lax.axis_size("blk")
    rows = residual.shape[0]
    mlp_in = rms_scale(residual, mlp_gain)
    spread = jnp.broadcast_to(mlp_in[None], (n_blk,) + mlp_in.shape)
    gathered = lax.all_to_all(spread, "blk", split_axis=0, concat_axis=0, tiled=True)
    gate_and_up = jnp.einsum(
        "nd,dkf->nkf",
        gathered.reshape(n_blk * rows, -1),
        all_weights[:, :2, :],
        preferred_element_type=jnp.float32,
    )
    hidden = (jax.nn.silu(gate_and_up[:, 0, :]) * gate_and_up[:, 1, :]).astype(jnp.bfloat16)
    partial = jnp.einsum(
        "nf,df->nd", hidden, all_weights[:, 2, :], preferred_element_type=jnp.float32
    ).astype(jnp.bfloat16)
    returned = lax.all_to_all(
        partial.reshape(n_blk, rows, -1), "blk", split_axis=0, concat_axis=0, tiled=True
    )
    mlp_rows = jnp.sum(returned.astype(jnp.float32), axis=0)
    return (residual + mlp_rows).astype(jnp.bfloat16)


def feed_forward_finish(residual, partial):
    mlp_rows = lax.psum_scatter(partial, "blk", scatter_dimension=0, tiled=True)
    return (residual + mlp_rows.astype(jnp.float32)).astype(jnp.bfloat16)


def solution(mesh):
    req_size = mesh.shape["req"]
    split_mesh = jax.sharding.Mesh(
        mesh.devices.reshape(req_size // 2, 2, mesh.shape["blk"]), ("zx", "core", "blk")
    )
    return jax.shard_map(
        shards,
        mesh=split_mesh,
        in_specs=(
            P("blk", REQ, None, None),
            P("blk", REQ, None, None),
            P("blk", REQ, None, None, None),
            P("blk", REQ, None, None),
            P("blk", REQ, None),
            P("blk", REQ, None),
            P(),
            P(),
            P(),
            P(),
            P(),
            P(REQ, None, "blk"),
            P("blk", REQ),
        ),
        out_specs=(
            P("blk", REQ, None, None),
            P("blk", REQ, None, None),
            P("blk", REQ, None, None, None),
        ),
        check_vma=False,
    )
```

```python
import math

import jax
import jax.numpy as jnp
from jax import lax
from jax.experimental import pallas as pl
from jax.experimental.pallas import tpu as pltpu
from jax.sharding import PartitionSpec as P

QUERY_HEADS = 12
KEY_VALUE_HEADS = 2
HEAD_SIZE = 128
CAP = 2


rms_eps = 1e-06
rope_base = 1000000.0


def rms_scale(rows, gain_row):
    rows_wide = rows.astype(jnp.float32)
    inverse = lax.rsqrt(jnp.mean(rows_wide * rows_wide, axis=-1, keepdims=True) + rms_eps)
    return (rows_wide * inverse * gain_row.astype(jnp.float32)).astype(jnp.bfloat16)


def apply_rotary(vectors, token_positions):
    head_dim = vectors.shape[-1]
    half_dim = head_dim // 2
    frequency = rope_base ** (-2.0 * jnp.arange(half_dim, dtype=jnp.float32) / head_dim)
    angles = token_positions.astype(jnp.float32)[:, None] * frequency[None, :]
    cosine = jnp.concatenate([jnp.cos(angles), jnp.cos(angles)], axis=-1)[:, None, :]
    sine_table = jnp.concatenate([jnp.sin(angles), jnp.sin(angles)], axis=-1)[:, None, :]
    turned = jnp.concatenate([-vectors[..., half_dim:], vectors[..., :half_dim]], axis=-1)
    return vectors * cosine + turned * sine_table


def project(normed, weight, bias_row, token_positions):
    mixed_batch = jnp.dot(normed, weight, preferred_element_type=jnp.float32) + bias_row.astype(
        jnp.float32
    )
    query_head_width = QUERY_HEADS * HEAD_SIZE
    key_head_width = KEY_VALUE_HEADS * HEAD_SIZE
    query_rows = apply_rotary(
        mixed_batch[:, :query_head_width].reshape(-1, QUERY_HEADS, HEAD_SIZE), token_positions
    )
    key_row_block = apply_rotary(
        mixed_batch[:, query_head_width : query_head_width + key_head_width].reshape(
            -1, KEY_VALUE_HEADS, HEAD_SIZE
        ),
        token_positions,
    )
    value_rows = mixed_batch[:, query_head_width + key_head_width :]
    key_value_pair = jnp.concatenate(
        [key_row_block.reshape(-1, key_head_width), value_rows], axis=-1
    )
    return (
        query_rows.reshape(-1, query_head_width).astype(jnp.bfloat16),
        key_value_pair.astype(jnp.bfloat16),
    )


def attend(query_rows, key_value_pair, allowed):
    batch_count = query_rows.shape[0]
    total_rows = query_rows.shape[1]
    group_width = QUERY_HEADS // KEY_VALUE_HEADS
    key_head_width = KEY_VALUE_HEADS * HEAD_SIZE
    grouped_heads = query_rows.reshape(
        batch_count, total_rows, KEY_VALUE_HEADS, group_width, HEAD_SIZE
    )
    key_row_block = key_value_pair[:, :, :key_head_width].reshape(
        batch_count, -1, KEY_VALUE_HEADS, HEAD_SIZE
    )
    value_rows = key_value_pair[:, :, key_head_width:].reshape(
        batch_count, -1, KEY_VALUE_HEADS, HEAD_SIZE
    )
    scores = jnp.einsum(
        "bqhgd,bkhd->bhgqk", grouped_heads, key_row_block, preferred_element_type=jnp.float32
    ) / math.sqrt(HEAD_SIZE)
    scores = jnp.where(allowed[:, None, None, :, :], scores, -jnp.inf)
    row_max = jnp.max(scores, axis=-1, keepdims=True)
    weights = jnp.exp(scores - row_max)
    weights = (weights / jnp.sum(weights, axis=-1, keepdims=True)).astype(jnp.bfloat16)
    result = jnp.einsum(
        "bhgqk,bkhd->bqhgd", weights, value_rows, preferred_element_type=jnp.float32
    )
    return result.reshape(batch_count, total_rows, QUERY_HEADS * HEAD_SIZE).astype(jnp.bfloat16)


def decode_kernel(order_ref, length_ref, cache_ref, kv_ref, q_ref, new_ref, att_ref):
    limit = length_ref[pl.program_id(0)]
    rows = cache_ref[...]
    positions = lax.broadcasted_iota(jnp.int32, rows.shape, 0)
    extended = jnp.where(
        positions < limit,
        rows,
        jnp.where(positions == limit, kv_ref[...], jnp.zeros_like(rows)),
    )
    new_ref[...] = extended
    group_width = QUERY_HEADS // KEY_VALUE_HEADS
    key_head_width = KEY_VALUE_HEADS * HEAD_SIZE
    key_ids = lax.broadcasted_iota(jnp.int32, (group_width, rows.shape[0]), 1)
    for head in range(KEY_VALUE_HEADS):
        keys = extended[:, head * HEAD_SIZE : (head + 1) * HEAD_SIZE]
        values = extended[:, key_head_width + head * HEAD_SIZE : key_head_width + (head + 1) * HEAD_SIZE]
        scores = lax.dot_general(
            q_ref[head], keys, (((1,), (1,)), ((), ())), preferred_element_type=jnp.float32
        ) / math.sqrt(HEAD_SIZE)
        scores = jnp.where(key_ids <= limit, scores, -jnp.inf)
        weights = jnp.exp(scores - jnp.max(scores, axis=1, keepdims=True))
        weights = (weights / jnp.sum(weights, axis=1, keepdims=True)).astype(jnp.bfloat16)
        att_ref[head] = jnp.dot(weights, values, preferred_element_type=jnp.float32).astype(
            jnp.bfloat16
        )


def decode_attend(arrival_order, got_length, recv_cache, decode_kv, decode_q, cache_length):
    count = arrival_order.shape[0]
    width_per_row = recv_cache.shape[2]
    group_width = QUERY_HEADS // KEY_VALUE_HEADS
    order = jnp.clip(arrival_order, 0, recv_cache.shape[0] - 1)
    new_cache, attended = pl.pallas_call(
        decode_kernel,
        grid_spec=pltpu.PrefetchScalarGridSpec(
            num_scalar_prefetch=2,
            grid=(count,),
            in_specs=[
                pl.BlockSpec((None, cache_length, width_per_row), lambda p, o, n: (o[p], 0, 0)),
                pl.BlockSpec((None, 1, width_per_row), lambda p, o, n: (p, 0, 0)),
                pl.BlockSpec(
                    (None, KEY_VALUE_HEADS, group_width, HEAD_SIZE), lambda p, o, n: (p, 0, 0, 0)
                ),
            ],
            out_specs=[
                pl.BlockSpec((None, cache_length, width_per_row), lambda p, o, n: (p, 0, 0)),
                pl.BlockSpec(
                    (None, KEY_VALUE_HEADS, group_width, HEAD_SIZE), lambda p, o, n: (p, 0, 0, 0)
                ),
            ],
        ),
        out_shape=[
            jax.ShapeDtypeStruct((count, cache_length, width_per_row), jnp.bfloat16),
            jax.ShapeDtypeStruct((count, KEY_VALUE_HEADS, group_width, HEAD_SIZE), jnp.bfloat16),
        ],
    )(
        order,
        got_length,
        recv_cache,
        decode_kv.reshape(count, 1, width_per_row),
        decode_q.reshape(count, KEY_VALUE_HEADS, group_width, HEAD_SIZE),
    )
    return new_cache, attended.reshape(count, QUERY_HEADS * HEAD_SIZE)


def extend(cache_rows, key_value_pair, lengths_now):
    token_positions = jnp.arange(cache_rows.shape[1], dtype=jnp.int32)[None, :, None]
    limit = lengths_now[:, None, None]
    return jnp.where(
        token_positions < limit,
        cache_rows,
        jnp.where(token_positions == limit, key_value_pair[:, None, :], jnp.zeros_like(cache_rows)),
    )


def shards(
    prefill_rows,
    decode_rows,
    cache_pool,
    page_table,
    lengths,
    destination,
    attn_gain,
    inproj_weight,
    inproj_bias,
    outproj_weight,
    mlp_gain,
    gate_up,
    down_weight,
):
    n_req = lax.axis_size("req")
    own_index = lax.axis_index("req")
    slot_total = destination.shape[2]
    pool_rows = cache_pool[0, 0]
    table_rows = page_table[0, 0]
    width_per_row = pool_rows.shape[-1]
    cache_length = table_rows.shape[1] * pool_rows.shape[1]
    context = pool_rows[table_rows[slot_total]].reshape(cache_length, width_per_row)
    context_length = lengths[0, 0, slot_total]
    slot_ids = jnp.arange(slot_total, dtype=jnp.int32)

    local_down = jnp.transpose(down_weight)[:, None, :]
    all_weights = lax.all_gather(
        jnp.concatenate([gate_up, local_down], axis=1), "req", axis=0, tiled=True
    )

    send_dest = destination[0, 0]
    decode_x = decode_rows[0, 0]
    own_len = lengths[0, 0, :slot_total]
    same_dest = send_dest[None, :] == send_dest[:, None]
    earlier = same_dest & (slot_ids[None, :] < slot_ids[:, None])
    within = jnp.sum(earlier.astype(jnp.int32), axis=1)
    target = send_dest * CAP + within
    flat_slots = jnp.arange(n_req * CAP, dtype=jnp.int32)
    matches = target[None, :] == flat_slots[:, None]
    picked = jnp.sum(jnp.where(matches, slot_ids[None, :], 0), axis=1)
    send_pages = table_rows[picked]
    send_count = n_req * CAP
    row_parts = decode_x.shape[1] // width_per_row
    sent_len = own_len[picked]
    length_code = jnp.stack([sent_len // 16, sent_len % 16], axis=1).astype(jnp.bfloat16)
    extra_rows = jnp.concatenate(
        [
            decode_x[picked].reshape(send_count, row_parts, width_per_row),
            jnp.pad(length_code, ((0, 0), (0, width_per_row - 2)))[:, None, :],
            jnp.zeros((send_count, 8 - row_parts - 1, width_per_row), jnp.bfloat16),
        ],
        axis=1,
    )
    send_cache = jnp.concatenate(
        [pool_rows[send_pages].reshape(send_count, cache_length, width_per_row), extra_rows],
        axis=1,
    ).reshape(n_req, CAP, cache_length + 8, width_per_row)

    shift = jnp.mod(send_dest - own_index, n_req)
    source = jnp.mod(own_index - shift, n_req)
    order_key = source * slot_total + slot_ids
    rank = jnp.sum((order_key[None, :] < order_key[:, None]).astype(jnp.int32), axis=1)
    chosen = rank[None, :] == slot_ids[:, None]
    arrival_order = jnp.sum(jnp.where(chosen, (source * CAP + within)[None, :], 0), axis=1)

    prefill_x = prefill_rows[0, 0]
    prefill_count = prefill_x.shape[0]
    block_ids = jnp.arange(prefill_count, dtype=jnp.int32)
    cache_ids = jnp.arange(cache_length, dtype=jnp.int32)
    prefill_q, prefill_kv = project(
        rms_scale(prefill_x, attn_gain), inproj_weight, inproj_bias, context_length + block_ids
    )
    key_block = jnp.concatenate([context, prefill_kv], axis=0)
    allowed = jnp.concatenate(
        [
            jnp.broadcast_to(cache_ids[None, :] < context_length, (prefill_count, cache_length)),
            block_ids[None, :] <= block_ids[:, None],
        ],
        axis=1,
    )
    prefill_att = attend(prefill_q[None], key_block[None], allowed[None])[0]
    prefill_res = prefill_x.astype(jnp.float32) + jnp.dot(
        prefill_att, outproj_weight, preferred_element_type=jnp.float32
    )
    all_weights, prefill_res, send_cache = lax.optimization_barrier(
        (all_weights, prefill_res, send_cache)
    )
    recv_cache = lax.all_to_all(send_cache, "req", split_axis=0, concat_axis=0, tiled=True)
    prefill_partial = feed_forward_partial(prefill_res, mlp_gain, all_weights)
    _, recv_cache = lax.optimization_barrier((prefill_partial, recv_cache))
    prefill_out = feed_forward_finish(prefill_res, prefill_partial)
    recv_cache = recv_cache.reshape(n_req * CAP, cache_length + 8, width_per_row)
    got_extra = recv_cache[arrival_order, cache_length:, :]
    got_x = got_extra[:, :row_parts, :].reshape(slot_total, -1)
    got_code = got_extra[:, row_parts, :2].astype(jnp.int32)
    got_length = got_code[:, 0] * 16 + got_code[:, 1]

    decode_q, decode_kv = project(
        rms_scale(got_x, attn_gain), inproj_weight, inproj_bias, got_length
    )
    cache_after, decode_att = decode_attend(
        arrival_order,
        got_length,
        recv_cache,
        decode_kv,
        decode_q,
        cache_length,
    )
    decode_res = got_x.astype(jnp.float32) + jnp.dot(
        decode_att, outproj_weight, preferred_element_type=jnp.float32
    )
    decode_out = small_feed_forward(decode_res, mlp_gain, all_weights)
    return (
        prefill_out[None, None],
        decode_out[None, None],
        cache_after[None, None],
    )


def feed_forward_partial(residual, mlp_gain, all_weights):
    mlp_in = rms_scale(residual, mlp_gain)
    gate_and_up = jnp.einsum(
        "nd,dkf->nkf",
        lax.all_gather(mlp_in, "blk", axis=0, tiled=True),
        all_weights[:, :2, :],
        preferred_element_type=jnp.float32,
    )
    hidden = (jax.nn.silu(gate_and_up[:, 0, :]) * gate_and_up[:, 1, :]).astype(jnp.bfloat16)
    return jnp.einsum(
        "nf,df->nd", hidden, all_weights[:, 2, :], preferred_element_type=jnp.float32
    ).astype(jnp.bfloat16)


def small_feed_forward(residual, mlp_gain, all_weights):
    n_blk = lax.axis_size("blk")
    rows = residual.shape[0]
    mlp_in = rms_scale(residual, mlp_gain)
    spread = jnp.broadcast_to(mlp_in[None], (n_blk,) + mlp_in.shape)
    gathered = lax.all_to_all(spread, "blk", split_axis=0, concat_axis=0, tiled=True)
    gate_and_up = jnp.einsum(
        "nd,dkf->nkf",
        gathered.reshape(n_blk * rows, -1),
        all_weights[:, :2, :],
        preferred_element_type=jnp.float32,
    )
    hidden = (jax.nn.silu(gate_and_up[:, 0, :]) * gate_and_up[:, 1, :]).astype(jnp.bfloat16)
    partial = jnp.einsum(
        "nf,df->nd", hidden, all_weights[:, 2, :], preferred_element_type=jnp.float32
    ).astype(jnp.bfloat16)
    returned = lax.all_to_all(
        partial.reshape(n_blk, rows, -1), "blk", split_axis=0, concat_axis=0, tiled=True
    )
    mlp_rows = jnp.sum(returned.astype(jnp.float32), axis=0)
    return (residual + mlp_rows).astype(jnp.bfloat16)


def feed_forward_finish(residual, partial):
    mlp_rows = lax.psum_scatter(partial, "blk", scatter_dimension=0, tiled=True)
    return (residual + mlp_rows.astype(jnp.float32)).astype(jnp.bfloat16)


def solution(mesh):
    return jax.shard_map(
        shards,
        mesh=mesh,
        in_specs=(
            P("blk", "req", None, None),
            P("blk", "req", None, None),
            P("blk", "req", None, None, None),
            P("blk", "req", None, None),
            P("blk", "req", None),
            P("blk", "req", None),
            P(),
            P(),
            P(),
            P(),
            P(),
            P("req", None, "blk"),
            P("blk", "req"),
        ),
        out_specs=(
            P("blk", "req", None, None),
            P("blk", "req", None, None),
            P("blk", "req", None, None, None),
        ),
        check_vma=False,
    )
```

```python
import math

import jax
import jax.numpy as jnp
from jax import lax
from jax.experimental import pallas as pl
from jax.experimental.pallas import tpu as pltpu
from jax.sharding import PartitionSpec as P

QUERY_HEADS = 12
KEY_VALUE_HEADS = 2
HEAD_SIZE = 128
CAP = 2


rms_eps = 1e-06
rope_base = 1000000.0


def rms_scale(rows, gain_row):
    rows_wide = rows.astype(jnp.float32)
    inverse = lax.rsqrt(jnp.mean(rows_wide * rows_wide, axis=-1, keepdims=True) + rms_eps)
    return (rows_wide * inverse * gain_row.astype(jnp.float32)).astype(jnp.bfloat16)


def apply_rotary(vectors, token_positions):
    head_dim = vectors.shape[-1]
    half_dim = head_dim // 2
    frequency = rope_base ** (-2.0 * jnp.arange(half_dim, dtype=jnp.float32) / head_dim)
    angles = token_positions.astype(jnp.float32)[:, None] * frequency[None, :]
    cosine = jnp.concatenate([jnp.cos(angles), jnp.cos(angles)], axis=-1)[:, None, :]
    sine_table = jnp.concatenate([jnp.sin(angles), jnp.sin(angles)], axis=-1)[:, None, :]
    turned = jnp.concatenate([-vectors[..., half_dim:], vectors[..., :half_dim]], axis=-1)
    return vectors * cosine + turned * sine_table


def project(normed, weight, bias_row, token_positions):
    mixed_batch = jnp.dot(normed, weight, preferred_element_type=jnp.float32) + bias_row.astype(
        jnp.float32
    )
    query_head_width = QUERY_HEADS * HEAD_SIZE
    key_head_width = KEY_VALUE_HEADS * HEAD_SIZE
    query_rows = apply_rotary(
        mixed_batch[:, :query_head_width].reshape(-1, QUERY_HEADS, HEAD_SIZE), token_positions
    )
    key_row_block = apply_rotary(
        mixed_batch[:, query_head_width : query_head_width + key_head_width].reshape(
            -1, KEY_VALUE_HEADS, HEAD_SIZE
        ),
        token_positions,
    )
    value_rows = mixed_batch[:, query_head_width + key_head_width :]
    key_value_pair = jnp.concatenate(
        [key_row_block.reshape(-1, key_head_width), value_rows], axis=-1
    )
    return (
        query_rows.reshape(-1, query_head_width).astype(jnp.bfloat16),
        key_value_pair.astype(jnp.bfloat16),
    )


def attend(query_rows, key_value_pair, allowed):
    batch_count = query_rows.shape[0]
    total_rows = query_rows.shape[1]
    group_width = QUERY_HEADS // KEY_VALUE_HEADS
    key_head_width = KEY_VALUE_HEADS * HEAD_SIZE
    grouped_heads = query_rows.reshape(
        batch_count, total_rows, KEY_VALUE_HEADS, group_width, HEAD_SIZE
    )
    key_row_block = key_value_pair[:, :, :key_head_width].reshape(
        batch_count, -1, KEY_VALUE_HEADS, HEAD_SIZE
    )
    value_rows = key_value_pair[:, :, key_head_width:].reshape(
        batch_count, -1, KEY_VALUE_HEADS, HEAD_SIZE
    )
    scores = jnp.einsum(
        "bqhgd,bkhd->bhgqk", grouped_heads, key_row_block, preferred_element_type=jnp.float32
    ) / math.sqrt(HEAD_SIZE)
    scores = jnp.where(allowed[:, None, None, :, :], scores, -jnp.inf)
    row_max = jnp.max(scores, axis=-1, keepdims=True)
    weights = jnp.exp(scores - row_max)
    weights = (weights / jnp.sum(weights, axis=-1, keepdims=True)).astype(jnp.bfloat16)
    result = jnp.einsum(
        "bhgqk,bkhd->bqhgd", weights, value_rows, preferred_element_type=jnp.float32
    )
    return result.reshape(batch_count, total_rows, QUERY_HEADS * HEAD_SIZE).astype(jnp.bfloat16)


def decode_kernel(order_ref, length_ref, first_ref, second_ref, kv_ref, q_ref, new_ref, att_ref):
    group_width = QUERY_HEADS // KEY_VALUE_HEADS
    key_head_width = KEY_VALUE_HEADS * HEAD_SIZE
    for half, cache_ref in enumerate((first_ref, second_ref)):
        limit = length_ref[2 * pl.program_id(0) + half]
        rows = cache_ref[...]
        positions = lax.broadcasted_iota(jnp.int32, rows.shape, 0)
        extended = jnp.where(
            positions < limit,
            rows,
            jnp.where(positions == limit, kv_ref[half], jnp.zeros_like(rows)),
        )
        new_ref[half] = extended
        key_ids = lax.broadcasted_iota(jnp.int32, (group_width, rows.shape[0]), 1)
        for head in range(KEY_VALUE_HEADS):
            keys = extended[:, head * HEAD_SIZE : (head + 1) * HEAD_SIZE]
            values = extended[
                :, key_head_width + head * HEAD_SIZE : key_head_width + (head + 1) * HEAD_SIZE
            ]
            scores = lax.dot_general(
                q_ref[half, head], keys, (((1,), (1,)), ((), ())), preferred_element_type=jnp.float32
            ) / math.sqrt(HEAD_SIZE)
            scores = jnp.where(key_ids <= limit, scores, -jnp.inf)
            weights = jnp.exp(scores - jnp.max(scores, axis=1, keepdims=True))
            weights = (weights / jnp.sum(weights, axis=1, keepdims=True)).astype(jnp.bfloat16)
            att_ref[half, head] = jnp.dot(
                weights, values, preferred_element_type=jnp.float32
            ).astype(jnp.bfloat16)


def decode_attend(arrival_order, got_length, recv_cache, decode_kv, decode_q):
    count = arrival_order.shape[0]
    cache_length, width_per_row = recv_cache.shape[1:]
    group_width = QUERY_HEADS // KEY_VALUE_HEADS
    order = jnp.clip(arrival_order, 0, recv_cache.shape[0] - 1)
    head_block = (2, KEY_VALUE_HEADS, group_width, HEAD_SIZE)
    new_cache, attended = pl.pallas_call(
        decode_kernel,
        grid_spec=pltpu.PrefetchScalarGridSpec(
            num_scalar_prefetch=2,
            grid=(count // 2,),
            in_specs=[
                pl.BlockSpec((None, cache_length, width_per_row), lambda p, o, n: (o[2 * p], 0, 0)),
                pl.BlockSpec(
                    (None, cache_length, width_per_row), lambda p, o, n: (o[2 * p + 1], 0, 0)
                ),
                pl.BlockSpec((2, 1, width_per_row), lambda p, o, n: (p, 0, 0)),
                pl.BlockSpec(head_block, lambda p, o, n: (p, 0, 0, 0)),
            ],
            out_specs=[
                pl.BlockSpec((2, cache_length, width_per_row), lambda p, o, n: (p, 0, 0)),
                pl.BlockSpec(head_block, lambda p, o, n: (p, 0, 0, 0)),
            ],
        ),
        out_shape=[
            jax.ShapeDtypeStruct((count, cache_length, width_per_row), jnp.bfloat16),
            jax.ShapeDtypeStruct((count, KEY_VALUE_HEADS, group_width, HEAD_SIZE), jnp.bfloat16),
        ],
    )(
        order,
        got_length,
        recv_cache,
        recv_cache,
        decode_kv.reshape(count, 1, width_per_row),
        decode_q.reshape(count, KEY_VALUE_HEADS, group_width, HEAD_SIZE),
    )
    return new_cache, attended.reshape(count, QUERY_HEADS * HEAD_SIZE)


def extend(cache_rows, key_value_pair, lengths_now):
    token_positions = jnp.arange(cache_rows.shape[1], dtype=jnp.int32)[None, :, None]
    limit = lengths_now[:, None, None]
    return jnp.where(
        token_positions < limit,
        cache_rows,
        jnp.where(token_positions == limit, key_value_pair[:, None, :], jnp.zeros_like(cache_rows)),
    )


def shards(
    prefill_rows,
    decode_rows,
    cache_pool,
    page_table,
    lengths,
    destination,
    attn_gain,
    inproj_weight,
    inproj_bias,
    outproj_weight,
    mlp_gain,
    gate_up,
    down_weight,
):
    n_req = lax.axis_size("req")
    own_index = lax.axis_index("req")
    slot_total = destination.shape[2]
    pool_rows = cache_pool[0, 0]
    table_rows = page_table[0, 0]
    width_per_row = pool_rows.shape[-1]
    cache_length = table_rows.shape[1] * pool_rows.shape[1]
    context = pool_rows[table_rows[slot_total]].reshape(cache_length, width_per_row)
    context_length = lengths[0, 0, slot_total]
    slot_ids = jnp.arange(slot_total, dtype=jnp.int32)

    local_down = jnp.transpose(down_weight)[:, None, :]
    all_weights = lax.all_gather(
        jnp.concatenate([gate_up, local_down], axis=1), "req", axis=0, tiled=True
    )

    send_dest = destination[0, 0]
    decode_x = decode_rows[0, 0]
    own_len = lengths[0, 0, :slot_total]
    same_dest = send_dest[None, :] == send_dest[:, None]
    earlier = same_dest & (slot_ids[None, :] < slot_ids[:, None])
    within = jnp.sum(earlier.astype(jnp.int32), axis=1)
    target = send_dest * CAP + within
    flat_slots = jnp.arange(n_req * CAP, dtype=jnp.int32)
    matches = target[None, :] == flat_slots[:, None]
    picked = jnp.sum(jnp.where(matches, slot_ids[None, :], 0), axis=1)
    send_pages = table_rows[picked]
    send_cache = pool_rows[send_pages].reshape(n_req, CAP, cache_length, width_per_row)
    send_x = decode_x[picked].reshape(n_req, CAP, -1)
    send_len = jnp.broadcast_to(own_len[picked].reshape(n_req, CAP, 1), (n_req, CAP, 128))
    recv_x = lax.all_to_all(send_x, "req", split_axis=0, concat_axis=0, tiled=True)
    recv_len = lax.all_to_all(send_len, "req", split_axis=0, concat_axis=0, tiled=True)

    shift = jnp.mod(send_dest - own_index, n_req)
    source = jnp.mod(own_index - shift, n_req)
    order_key = source * slot_total + slot_ids
    rank = jnp.sum((order_key[None, :] < order_key[:, None]).astype(jnp.int32), axis=1)
    chosen = rank[None, :] == slot_ids[:, None]
    arrival_order = jnp.sum(jnp.where(chosen, (source * CAP + within)[None, :], 0), axis=1)

    prefill_x = prefill_rows[0, 0]
    prefill_count = prefill_x.shape[0]
    block_ids = jnp.arange(prefill_count, dtype=jnp.int32)
    cache_ids = jnp.arange(cache_length, dtype=jnp.int32)
    prefill_q, prefill_kv = project(
        rms_scale(prefill_x, attn_gain), inproj_weight, inproj_bias, context_length + block_ids
    )
    key_block = jnp.concatenate([context, prefill_kv], axis=0)
    allowed = jnp.concatenate(
        [
            jnp.broadcast_to(cache_ids[None, :] < context_length, (prefill_count, cache_length)),
            block_ids[None, :] <= block_ids[:, None],
        ],
        axis=1,
    )
    prefill_att = attend(prefill_q[None], key_block[None], allowed[None])[0]
    prefill_res = prefill_x.astype(jnp.float32) + jnp.dot(
        prefill_att, outproj_weight, preferred_element_type=jnp.float32
    )
    all_weights, prefill_res, send_cache = lax.optimization_barrier(
        (all_weights, prefill_res, send_cache)
    )
    recv_cache = lax.all_to_all(send_cache, "req", split_axis=0, concat_axis=0, tiled=True)
    prefill_partial = feed_forward_partial(prefill_res, mlp_gain, all_weights)
    _, recv_cache, recv_x, recv_len = lax.optimization_barrier(
        (prefill_partial, recv_cache, recv_x, recv_len)
    )
    prefill_out = feed_forward_finish(prefill_res, prefill_partial)
    got_x = recv_x.reshape(n_req * CAP, -1)[arrival_order]
    got_length = recv_len.reshape(n_req * CAP, 128)[arrival_order, 0]

    decode_q, decode_kv = project(
        rms_scale(got_x, attn_gain), inproj_weight, inproj_bias, got_length
    )
    cache_after, decode_att = decode_attend(
        arrival_order,
        got_length,
        recv_cache.reshape(n_req * CAP, cache_length, width_per_row),
        decode_kv,
        decode_q,
    )
    decode_res = got_x.astype(jnp.float32) + jnp.dot(
        decode_att, outproj_weight, preferred_element_type=jnp.float32
    )
    decode_out = small_feed_forward(decode_res, mlp_gain, all_weights)
    return (
        prefill_out[None, None],
        decode_out[None, None],
        cache_after[None, None],
    )


def feed_forward_partial(residual, mlp_gain, all_weights):
    mlp_in = rms_scale(residual, mlp_gain)
    gate_and_up = jnp.einsum(
        "nd,dkf->nkf",
        lax.all_gather(mlp_in, "blk", axis=0, tiled=True),
        all_weights[:, :2, :],
        preferred_element_type=jnp.float32,
    )
    hidden = (jax.nn.silu(gate_and_up[:, 0, :]) * gate_and_up[:, 1, :]).astype(jnp.bfloat16)
    return jnp.einsum(
        "nf,df->nd", hidden, all_weights[:, 2, :], preferred_element_type=jnp.float32
    ).astype(jnp.bfloat16)


def small_feed_forward(residual, mlp_gain, all_weights):
    n_blk = lax.axis_size("blk")
    rows = residual.shape[0]
    mlp_in = rms_scale(residual, mlp_gain)
    spread = jnp.broadcast_to(mlp_in[None], (n_blk,) + mlp_in.shape)
    gathered = lax.all_to_all(spread, "blk", split_axis=0, concat_axis=0, tiled=True)
    gate_and_up = jnp.einsum(
        "nd,dkf->nkf",
        gathered.reshape(n_blk * rows, -1),
        all_weights[:, :2, :],
        preferred_element_type=jnp.float32,
    )
    hidden = (jax.nn.silu(gate_and_up[:, 0, :]) * gate_and_up[:, 1, :]).astype(jnp.bfloat16)
    partial = jnp.einsum(
        "nf,df->nd", hidden, all_weights[:, 2, :], preferred_element_type=jnp.float32
    ).astype(jnp.bfloat16)
    returned = lax.all_to_all(
        partial.reshape(n_blk, rows, -1), "blk", split_axis=0, concat_axis=0, tiled=True
    )
    mlp_rows = jnp.sum(returned.astype(jnp.float32), axis=0)
    return (residual + mlp_rows).astype(jnp.bfloat16)


def feed_forward_finish(residual, partial):
    mlp_rows = lax.psum_scatter(partial, "blk", scatter_dimension=0, tiled=True)
    return (residual + mlp_rows.astype(jnp.float32)).astype(jnp.bfloat16)


def solution(mesh):
    return jax.shard_map(
        shards,
        mesh=mesh,
        in_specs=(
            P("blk", "req", None, None),
            P("blk", "req", None, None),
            P("blk", "req", None, None, None),
            P("blk", "req", None, None),
            P("blk", "req", None),
            P("blk", "req", None),
            P(),
            P(),
            P(),
            P(),
            P(),
            P("req", None, "blk"),
            P("blk", "req"),
        ),
        out_specs=(
            P("blk", "req", None, None),
            P("blk", "req", None, None),
            P("blk", "req", None, None, None),
        ),
        check_vma=False,
    )
```

```python
import math

import jax
import jax.numpy as jnp
from jax import lax
from jax.experimental import pallas as pl
from jax.experimental.pallas import tpu as pltpu
from jax.sharding import PartitionSpec as P

QUERY_HEADS = 12
KEY_VALUE_HEADS = 2
HEAD_SIZE = 128
CAP = 2


rms_eps = 1e-06
rope_base = 1000000.0


def rms_scale(rows, gain_row):
    rows_wide = rows.astype(jnp.float32)
    inverse = lax.rsqrt(jnp.mean(rows_wide * rows_wide, axis=-1, keepdims=True) + rms_eps)
    return (rows_wide * inverse * gain_row.astype(jnp.float32)).astype(jnp.bfloat16)


def apply_rotary(vectors, token_positions):
    head_dim = vectors.shape[-1]
    half_dim = head_dim // 2
    frequency = rope_base ** (-2.0 * jnp.arange(half_dim, dtype=jnp.float32) / head_dim)
    angles = token_positions.astype(jnp.float32)[:, None] * frequency[None, :]
    cosine = jnp.concatenate([jnp.cos(angles), jnp.cos(angles)], axis=-1)[:, None, :]
    sine_table = jnp.concatenate([jnp.sin(angles), jnp.sin(angles)], axis=-1)[:, None, :]
    turned = jnp.concatenate([-vectors[..., half_dim:], vectors[..., :half_dim]], axis=-1)
    return vectors * cosine + turned * sine_table


def project(normed, weight, bias_row, token_positions):
    mixed_batch = jnp.dot(normed, weight, preferred_element_type=jnp.float32) + bias_row.astype(
        jnp.float32
    )
    query_head_width = QUERY_HEADS * HEAD_SIZE
    key_head_width = KEY_VALUE_HEADS * HEAD_SIZE
    query_rows = apply_rotary(
        mixed_batch[:, :query_head_width].reshape(-1, QUERY_HEADS, HEAD_SIZE), token_positions
    )
    key_row_block = apply_rotary(
        mixed_batch[:, query_head_width : query_head_width + key_head_width].reshape(
            -1, KEY_VALUE_HEADS, HEAD_SIZE
        ),
        token_positions,
    )
    value_rows = mixed_batch[:, query_head_width + key_head_width :]
    key_value_pair = jnp.concatenate(
        [key_row_block.reshape(-1, key_head_width), value_rows], axis=-1
    )
    return (
        query_rows.reshape(-1, query_head_width).astype(jnp.bfloat16),
        key_value_pair.astype(jnp.bfloat16),
    )


def attend(query_rows, key_value_pair, allowed):
    batch_count = query_rows.shape[0]
    total_rows = query_rows.shape[1]
    group_width = QUERY_HEADS // KEY_VALUE_HEADS
    key_head_width = KEY_VALUE_HEADS * HEAD_SIZE
    grouped_heads = query_rows.reshape(
        batch_count, total_rows, KEY_VALUE_HEADS, group_width, HEAD_SIZE
    )
    key_row_block = key_value_pair[:, :, :key_head_width].reshape(
        batch_count, -1, KEY_VALUE_HEADS, HEAD_SIZE
    )
    value_rows = key_value_pair[:, :, key_head_width:].reshape(
        batch_count, -1, KEY_VALUE_HEADS, HEAD_SIZE
    )
    scores = jnp.einsum(
        "bqhgd,bkhd->bhgqk", grouped_heads, key_row_block, preferred_element_type=jnp.float32
    ) / math.sqrt(HEAD_SIZE)
    scores = jnp.where(allowed[:, None, None, :, :], scores, -jnp.inf)
    row_max = jnp.max(scores, axis=-1, keepdims=True)
    weights = jnp.exp(scores - row_max)
    weights = (weights / jnp.sum(weights, axis=-1, keepdims=True)).astype(jnp.bfloat16)
    result = jnp.einsum(
        "bhgqk,bkhd->bqhgd", weights, value_rows, preferred_element_type=jnp.float32
    )
    return result.reshape(batch_count, total_rows, QUERY_HEADS * HEAD_SIZE).astype(jnp.bfloat16)


def decode_kernel(order_ref, length_ref, first_ref, second_ref, kv_ref, q_ref, new_ref, att_ref):
    group_width = QUERY_HEADS // KEY_VALUE_HEADS
    key_head_width = KEY_VALUE_HEADS * HEAD_SIZE
    for half, cache_ref in enumerate((first_ref, second_ref)):
        limit = length_ref[2 * pl.program_id(0) + half]
        rows = cache_ref[...]
        positions = lax.broadcasted_iota(jnp.int32, rows.shape, 0)
        extended = jnp.where(
            positions < limit,
            rows,
            jnp.where(positions == limit, kv_ref[half], jnp.zeros_like(rows)),
        )
        new_ref[half] = extended
        key_ids = lax.broadcasted_iota(jnp.int32, (group_width, rows.shape[0]), 1)
        for head in range(KEY_VALUE_HEADS):
            keys = extended[:, head * HEAD_SIZE : (head + 1) * HEAD_SIZE]
            values = extended[
                :, key_head_width + head * HEAD_SIZE : key_head_width + (head + 1) * HEAD_SIZE
            ]
            scores = lax.dot_general(
                q_ref[half, head], keys, (((1,), (1,)), ((), ())), preferred_element_type=jnp.float32
            ) / math.sqrt(HEAD_SIZE)
            scores = jnp.where(key_ids <= limit, scores, -jnp.inf)
            weights = jnp.exp(scores - jnp.max(scores, axis=1, keepdims=True))
            weights = (weights / jnp.sum(weights, axis=1, keepdims=True)).astype(jnp.bfloat16)
            att_ref[half, head] = jnp.dot(
                weights, values, preferred_element_type=jnp.float32
            ).astype(jnp.bfloat16)


def decode_attend(arrival_order, got_length, recv_cache, decode_kv, decode_q):
    count = arrival_order.shape[0]
    cache_length, width_per_row = recv_cache.shape[1:]
    group_width = QUERY_HEADS // KEY_VALUE_HEADS
    order = jnp.clip(arrival_order, 0, recv_cache.shape[0] - 1)
    head_block = (2, KEY_VALUE_HEADS, group_width, HEAD_SIZE)
    new_cache, attended = pl.pallas_call(
        decode_kernel,
        grid_spec=pltpu.PrefetchScalarGridSpec(
            num_scalar_prefetch=2,
            grid=(count // 2,),
            in_specs=[
                pl.BlockSpec((None, cache_length, width_per_row), lambda p, o, n: (o[2 * p], 0, 0)),
                pl.BlockSpec(
                    (None, cache_length, width_per_row), lambda p, o, n: (o[2 * p + 1], 0, 0)
                ),
                pl.BlockSpec((2, 1, width_per_row), lambda p, o, n: (p, 0, 0)),
                pl.BlockSpec(head_block, lambda p, o, n: (p, 0, 0, 0)),
            ],
            out_specs=[
                pl.BlockSpec((2, cache_length, width_per_row), lambda p, o, n: (p, 0, 0)),
                pl.BlockSpec(head_block, lambda p, o, n: (p, 0, 0, 0)),
            ],
        ),
        out_shape=[
            jax.ShapeDtypeStruct((count, cache_length, width_per_row), jnp.bfloat16),
            jax.ShapeDtypeStruct((count, KEY_VALUE_HEADS, group_width, HEAD_SIZE), jnp.bfloat16),
        ],
    )(
        order,
        got_length,
        recv_cache,
        recv_cache,
        decode_kv.reshape(count, 1, width_per_row),
        decode_q.reshape(count, KEY_VALUE_HEADS, group_width, HEAD_SIZE),
    )
    return new_cache, attended.reshape(count, QUERY_HEADS * HEAD_SIZE)


def extend(cache_rows, key_value_pair, lengths_now):
    token_positions = jnp.arange(cache_rows.shape[1], dtype=jnp.int32)[None, :, None]
    limit = lengths_now[:, None, None]
    return jnp.where(
        token_positions < limit,
        cache_rows,
        jnp.where(token_positions == limit, key_value_pair[:, None, :], jnp.zeros_like(cache_rows)),
    )


def shards(
    prefill_rows,
    decode_rows,
    cache_pool,
    page_table,
    lengths,
    destination,
    attn_gain,
    inproj_weight,
    inproj_bias,
    outproj_weight,
    mlp_gain,
    gate_up,
    down_weight,
):
    n_req = lax.axis_size("req")
    own_index = lax.axis_index("req")
    slot_total = destination.shape[2]
    pool_rows = cache_pool[0, 0]
    table_rows = page_table[0, 0]
    width_per_row = pool_rows.shape[-1]
    cache_length = table_rows.shape[1] * pool_rows.shape[1]
    context = pool_rows[table_rows[slot_total]].reshape(cache_length, width_per_row)
    context_length = lengths[0, 0, slot_total]
    slot_ids = jnp.arange(slot_total, dtype=jnp.int32)

    local_down = jnp.transpose(down_weight)[:, None, :]
    all_weights = lax.all_gather(
        jnp.concatenate([gate_up, local_down], axis=1), "req", axis=0, tiled=True
    )

    send_dest = destination[0, 0]
    decode_x = decode_rows[0, 0]
    own_len = lengths[0, 0, :slot_total]
    same_dest = send_dest[None, :] == send_dest[:, None]
    earlier = same_dest & (slot_ids[None, :] < slot_ids[:, None])
    within = jnp.sum(earlier.astype(jnp.int32), axis=1)
    target = send_dest * CAP + within
    flat_slots = jnp.arange(n_req * CAP, dtype=jnp.int32)
    matches = target[None, :] == flat_slots[:, None]
    picked = jnp.sum(jnp.where(matches, slot_ids[None, :], 0), axis=1)
    send_pages = table_rows[picked]
    send_cache = pool_rows[send_pages].reshape(n_req, CAP, cache_length, width_per_row)
    sent_len = own_len[picked]
    length_code = jnp.stack([sent_len // 16, sent_len % 16], axis=1).astype(jnp.bfloat16)
    send_x = jnp.concatenate(
        [decode_x[picked], jnp.pad(length_code, ((0, 0), (0, 126)))], axis=1
    ).reshape(n_req, CAP, -1)
    recv_x = lax.all_to_all(send_x, "req", split_axis=0, concat_axis=0, tiled=True)

    shift = jnp.mod(send_dest - own_index, n_req)
    source = jnp.mod(own_index - shift, n_req)
    order_key = source * slot_total + slot_ids
    rank = jnp.sum((order_key[None, :] < order_key[:, None]).astype(jnp.int32), axis=1)
    chosen = rank[None, :] == slot_ids[:, None]
    arrival_order = jnp.sum(jnp.where(chosen, (source * CAP + within)[None, :], 0), axis=1)

    prefill_x = prefill_rows[0, 0]
    prefill_count = prefill_x.shape[0]
    block_ids = jnp.arange(prefill_count, dtype=jnp.int32)
    cache_ids = jnp.arange(cache_length, dtype=jnp.int32)
    prefill_q, prefill_kv = project(
        rms_scale(prefill_x, attn_gain), inproj_weight, inproj_bias, context_length + block_ids
    )
    key_block = jnp.concatenate([context, prefill_kv], axis=0)
    allowed = jnp.concatenate(
        [
            jnp.broadcast_to(cache_ids[None, :] < context_length, (prefill_count, cache_length)),
            block_ids[None, :] <= block_ids[:, None],
        ],
        axis=1,
    )
    prefill_att = attend(prefill_q[None], key_block[None], allowed[None])[0]
    prefill_res = prefill_x.astype(jnp.float32) + jnp.dot(
        prefill_att, outproj_weight, preferred_element_type=jnp.float32
    )
    all_weights, prefill_res, send_cache = lax.optimization_barrier(
        (all_weights, prefill_res, send_cache)
    )
    recv_cache = lax.all_to_all(send_cache, "req", split_axis=0, concat_axis=0, tiled=True)
    prefill_partial = feed_forward_partial(prefill_res, mlp_gain, all_weights)
    _, recv_cache, recv_x = lax.optimization_barrier((prefill_partial, recv_cache, recv_x))
    prefill_out = feed_forward_finish(prefill_res, prefill_partial)
    got_row = recv_x.reshape(n_req * CAP, -1)[arrival_order]
    got_x = got_row[:, : decode_x.shape[1]]
    got_code = got_row[:, decode_x.shape[1] : decode_x.shape[1] + 2].astype(jnp.int32)
    got_length = got_code[:, 0] * 16 + got_code[:, 1]

    decode_q, decode_kv = project(
        rms_scale(got_x, attn_gain), inproj_weight, inproj_bias, got_length
    )
    cache_after, decode_att = decode_attend(
        arrival_order,
        got_length,
        recv_cache.reshape(n_req * CAP, cache_length, width_per_row),
        decode_kv,
        decode_q,
    )
    decode_res = got_x.astype(jnp.float32) + jnp.dot(
        decode_att, outproj_weight, preferred_element_type=jnp.float32
    )
    decode_out = small_feed_forward(decode_res, mlp_gain, all_weights)
    return (
        prefill_out[None, None],
        decode_out[None, None],
        cache_after[None, None],
    )


def feed_forward_partial(residual, mlp_gain, all_weights):
    mlp_in = rms_scale(residual, mlp_gain)
    gate_and_up = jnp.einsum(
        "nd,dkf->nkf",
        lax.all_gather(mlp_in, "blk", axis=0, tiled=True),
        all_weights[:, :2, :],
        preferred_element_type=jnp.float32,
    )
    hidden = (jax.nn.silu(gate_and_up[:, 0, :]) * gate_and_up[:, 1, :]).astype(jnp.bfloat16)
    return jnp.einsum(
        "nf,df->nd", hidden, all_weights[:, 2, :], preferred_element_type=jnp.float32
    ).astype(jnp.bfloat16)


def small_feed_forward(residual, mlp_gain, all_weights):
    n_blk = lax.axis_size("blk")
    rows = residual.shape[0]
    mlp_in = rms_scale(residual, mlp_gain)
    spread = jnp.broadcast_to(mlp_in[None], (n_blk,) + mlp_in.shape)
    gathered = lax.all_to_all(spread, "blk", split_axis=0, concat_axis=0, tiled=True)
    gate_and_up = jnp.einsum(
        "nd,dkf->nkf",
        gathered.reshape(n_blk * rows, -1),
        all_weights[:, :2, :],
        preferred_element_type=jnp.float32,
    )
    hidden = (jax.nn.silu(gate_and_up[:, 0, :]) * gate_and_up[:, 1, :]).astype(jnp.bfloat16)
    partial = jnp.einsum(
        "nf,df->nd", hidden, all_weights[:, 2, :], preferred_element_type=jnp.float32
    ).astype(jnp.bfloat16)
    returned = lax.all_to_all(
        partial.reshape(n_blk, rows, -1), "blk", split_axis=0, concat_axis=0, tiled=True
    )
    mlp_rows = jnp.sum(returned.astype(jnp.float32), axis=0)
    return (residual + mlp_rows).astype(jnp.bfloat16)


def feed_forward_finish(residual, partial):
    mlp_rows = lax.psum_scatter(partial, "blk", scatter_dimension=0, tiled=True)
    return (residual + mlp_rows.astype(jnp.float32)).astype(jnp.bfloat16)


def solution(mesh):
    return jax.shard_map(
        shards,
        mesh=mesh,
        in_specs=(
            P("blk", "req", None, None),
            P("blk", "req", None, None),
            P("blk", "req", None, None, None),
            P("blk", "req", None, None),
            P("blk", "req", None),
            P("blk", "req", None),
            P(),
            P(),
            P(),
            P(),
            P(),
            P("req", None, "blk"),
            P("blk", "req"),
        ),
        out_specs=(
            P("blk", "req", None, None),
            P("blk", "req", None, None),
            P("blk", "req", None, None, None),
        ),
        check_vma=False,
    )
```

```python
import math

import jax
import jax.numpy as jnp
from jax import lax
from jax.experimental import pallas as pl
from jax.experimental.pallas import tpu as pltpu
from jax.sharding import PartitionSpec as P

QUERY_HEADS = 12
KEY_VALUE_HEADS = 2
HEAD_SIZE = 128
CAP = 2


rms_eps = 1e-06
rope_base = 1000000.0


def rms_scale(rows, gain_row):
    rows_wide = rows.astype(jnp.float32)
    inverse = lax.rsqrt(jnp.mean(rows_wide * rows_wide, axis=-1, keepdims=True) + rms_eps)
    return (rows_wide * inverse * gain_row.astype(jnp.float32)).astype(jnp.bfloat16)


def apply_rotary(vectors, token_positions):
    head_dim = vectors.shape[-1]
    half_dim = head_dim // 2
    frequency = rope_base ** (-2.0 * jnp.arange(half_dim, dtype=jnp.float32) / head_dim)
    angles = token_positions.astype(jnp.float32)[:, None] * frequency[None, :]
    cosine = jnp.concatenate([jnp.cos(angles), jnp.cos(angles)], axis=-1)[:, None, :]
    sine_table = jnp.concatenate([jnp.sin(angles), jnp.sin(angles)], axis=-1)[:, None, :]
    turned = jnp.concatenate([-vectors[..., half_dim:], vectors[..., :half_dim]], axis=-1)
    return vectors * cosine + turned * sine_table


def project(normed, weight, bias_row, token_positions):
    mixed_batch = jnp.dot(normed, weight, preferred_element_type=jnp.float32) + bias_row.astype(
        jnp.float32
    )
    query_head_width = QUERY_HEADS * HEAD_SIZE
    key_head_width = KEY_VALUE_HEADS * HEAD_SIZE
    query_rows = apply_rotary(
        mixed_batch[:, :query_head_width].reshape(-1, QUERY_HEADS, HEAD_SIZE), token_positions
    )
    key_row_block = apply_rotary(
        mixed_batch[:, query_head_width : query_head_width + key_head_width].reshape(
            -1, KEY_VALUE_HEADS, HEAD_SIZE
        ),
        token_positions,
    )
    value_rows = mixed_batch[:, query_head_width + key_head_width :]
    key_value_pair = jnp.concatenate(
        [key_row_block.reshape(-1, key_head_width), value_rows], axis=-1
    )
    return (
        query_rows.reshape(-1, query_head_width).astype(jnp.bfloat16),
        key_value_pair.astype(jnp.bfloat16),
    )


def attend(query_rows, key_value_pair, allowed):
    batch_count = query_rows.shape[0]
    total_rows = query_rows.shape[1]
    group_width = QUERY_HEADS // KEY_VALUE_HEADS
    key_head_width = KEY_VALUE_HEADS * HEAD_SIZE
    grouped_heads = query_rows.reshape(
        batch_count, total_rows, KEY_VALUE_HEADS, group_width, HEAD_SIZE
    )
    key_row_block = key_value_pair[:, :, :key_head_width].reshape(
        batch_count, -1, KEY_VALUE_HEADS, HEAD_SIZE
    )
    value_rows = key_value_pair[:, :, key_head_width:].reshape(
        batch_count, -1, KEY_VALUE_HEADS, HEAD_SIZE
    )
    scores = jnp.einsum(
        "bqhgd,bkhd->bhgqk", grouped_heads, key_row_block, preferred_element_type=jnp.float32
    ) / math.sqrt(HEAD_SIZE)
    scores = jnp.where(allowed[:, None, None, :, :], scores, -jnp.inf)
    row_max = jnp.max(scores, axis=-1, keepdims=True)
    weights = jnp.exp(scores - row_max)
    weights = (weights / jnp.sum(weights, axis=-1, keepdims=True)).astype(jnp.bfloat16)
    result = jnp.einsum(
        "bhgqk,bkhd->bqhgd", weights, value_rows, preferred_element_type=jnp.float32
    )
    return result.reshape(batch_count, total_rows, QUERY_HEADS * HEAD_SIZE).astype(jnp.bfloat16)


def decode_kernel(order_ref, length_ref, first_ref, second_ref, kv_ref, q_ref, new_ref, att_ref):
    group_width = QUERY_HEADS // KEY_VALUE_HEADS
    key_head_width = KEY_VALUE_HEADS * HEAD_SIZE
    for half, cache_ref in enumerate((first_ref, second_ref)):
        limit = length_ref[2 * pl.program_id(0) + half]
        rows = cache_ref[...]
        positions = lax.broadcasted_iota(jnp.int32, rows.shape, 0)
        extended = jnp.where(
            positions < limit,
            rows,
            jnp.where(positions == limit, kv_ref[half], jnp.zeros_like(rows)),
        )
        new_ref[half] = extended
        key_ids = lax.broadcasted_iota(jnp.int32, (group_width, rows.shape[0]), 1)
        for head in range(KEY_VALUE_HEADS):
            keys = extended[:, head * HEAD_SIZE : (head + 1) * HEAD_SIZE]
            values = extended[
                :, key_head_width + head * HEAD_SIZE : key_head_width + (head + 1) * HEAD_SIZE
            ]
            scores = lax.dot_general(
                q_ref[half, head], keys, (((1,), (1,)), ((), ())), preferred_element_type=jnp.float32
            ) / math.sqrt(HEAD_SIZE)
            scores = jnp.where(key_ids <= limit, scores, -jnp.inf)
            weights = jnp.exp(scores - jnp.max(scores, axis=1, keepdims=True))
            weights = (weights / jnp.sum(weights, axis=1, keepdims=True)).astype(jnp.bfloat16)
            att_ref[half, head] = jnp.dot(
                weights, values, preferred_element_type=jnp.float32
            ).astype(jnp.bfloat16)


def decode_attend(arrival_order, got_length, recv_cache, decode_kv, decode_q):
    count = arrival_order.shape[0]
    cache_length, width_per_row = recv_cache.shape[1:]
    group_width = QUERY_HEADS // KEY_VALUE_HEADS
    order = jnp.clip(arrival_order, 0, recv_cache.shape[0] - 1)
    head_block = (2, KEY_VALUE_HEADS, group_width, HEAD_SIZE)
    new_cache, attended = pl.pallas_call(
        decode_kernel,
        grid_spec=pltpu.PrefetchScalarGridSpec(
            num_scalar_prefetch=2,
            grid=(count // 2,),
            in_specs=[
                pl.BlockSpec((None, cache_length, width_per_row), lambda p, o, n: (o[2 * p], 0, 0)),
                pl.BlockSpec(
                    (None, cache_length, width_per_row), lambda p, o, n: (o[2 * p + 1], 0, 0)
                ),
                pl.BlockSpec((2, 1, width_per_row), lambda p, o, n: (p, 0, 0)),
                pl.BlockSpec(head_block, lambda p, o, n: (p, 0, 0, 0)),
            ],
            out_specs=[
                pl.BlockSpec((2, cache_length, width_per_row), lambda p, o, n: (p, 0, 0)),
                pl.BlockSpec(head_block, lambda p, o, n: (p, 0, 0, 0)),
            ],
        ),
        out_shape=[
            jax.ShapeDtypeStruct((count, cache_length, width_per_row), jnp.bfloat16),
            jax.ShapeDtypeStruct((count, KEY_VALUE_HEADS, group_width, HEAD_SIZE), jnp.bfloat16),
        ],
    )(
        order,
        got_length,
        recv_cache,
        recv_cache,
        decode_kv.reshape(count, 1, width_per_row),
        decode_q.reshape(count, KEY_VALUE_HEADS, group_width, HEAD_SIZE),
    )
    return new_cache, attended.reshape(count, QUERY_HEADS * HEAD_SIZE)


def extend(cache_rows, key_value_pair, lengths_now):
    token_positions = jnp.arange(cache_rows.shape[1], dtype=jnp.int32)[None, :, None]
    limit = lengths_now[:, None, None]
    return jnp.where(
        token_positions < limit,
        cache_rows,
        jnp.where(token_positions == limit, key_value_pair[:, None, :], jnp.zeros_like(cache_rows)),
    )


def shards(
    prefill_rows,
    decode_rows,
    cache_pool,
    page_table,
    lengths,
    destination,
    attn_gain,
    inproj_weight,
    inproj_bias,
    outproj_weight,
    mlp_gain,
    gate_up,
    down_weight,
):
    n_req = lax.axis_size("req")
    own_index = lax.axis_index("req")
    slot_total = destination.shape[2]
    pool_rows = cache_pool[0, 0]
    table_rows = page_table[0, 0]
    width_per_row = pool_rows.shape[-1]
    cache_length = table_rows.shape[1] * pool_rows.shape[1]
    context = pool_rows[table_rows[slot_total]].reshape(cache_length, width_per_row)
    context_length = lengths[0, 0, slot_total]
    slot_ids = jnp.arange(slot_total, dtype=jnp.int32)

    local_down = jnp.transpose(down_weight)[:, None, :]
    all_weights = lax.all_gather(
        jnp.concatenate([gate_up, local_down], axis=1), "req", axis=0, tiled=True
    )

    send_dest = destination[0, 0]
    decode_x = decode_rows[0, 0]
    own_len = lengths[0, 0, :slot_total]
    same_dest = send_dest[None, :] == send_dest[:, None]
    earlier = same_dest & (slot_ids[None, :] < slot_ids[:, None])
    within = jnp.sum(earlier.astype(jnp.int32), axis=1)
    target = send_dest * CAP + within
    flat_slots = jnp.arange(n_req * CAP, dtype=jnp.int32)
    matches = target[None, :] == flat_slots[:, None]
    picked = jnp.sum(jnp.where(matches, slot_ids[None, :], 0), axis=1)
    send_pages = table_rows[picked]
    send_cache = pool_rows[send_pages].reshape(n_req, CAP, cache_length, width_per_row)
    sent_len = own_len
    length_code = jnp.stack([sent_len // 16, sent_len % 16], axis=1).astype(jnp.bfloat16)
    coded_rows = jnp.concatenate(
        [decode_x, jnp.pad(length_code, ((0, 0), (0, 126)))], axis=1
    )
    recv_x = lax.all_gather(coded_rows, "req", axis=0, tiled=True)

    shift = jnp.mod(send_dest - own_index, n_req)
    source = jnp.mod(own_index - shift, n_req)
    order_key = source * slot_total + slot_ids
    rank = jnp.sum((order_key[None, :] < order_key[:, None]).astype(jnp.int32), axis=1)
    chosen = rank[None, :] == slot_ids[:, None]
    arrival_order = jnp.sum(jnp.where(chosen, (source * CAP + within)[None, :], 0), axis=1)

    prefill_x = prefill_rows[0, 0]
    prefill_count = prefill_x.shape[0]
    block_ids = jnp.arange(prefill_count, dtype=jnp.int32)
    cache_ids = jnp.arange(cache_length, dtype=jnp.int32)
    prefill_q, prefill_kv = project(
        rms_scale(prefill_x, attn_gain), inproj_weight, inproj_bias, context_length + block_ids
    )
    key_block = jnp.concatenate([context, prefill_kv], axis=0)
    allowed = jnp.concatenate(
        [
            jnp.broadcast_to(cache_ids[None, :] < context_length, (prefill_count, cache_length)),
            block_ids[None, :] <= block_ids[:, None],
        ],
        axis=1,
    )
    prefill_att = attend(prefill_q[None], key_block[None], allowed[None])[0]
    prefill_res = prefill_x.astype(jnp.float32) + jnp.dot(
        prefill_att, outproj_weight, preferred_element_type=jnp.float32
    )
    all_weights, prefill_res, send_cache = lax.optimization_barrier(
        (all_weights, prefill_res, send_cache)
    )
    recv_cache = lax.all_to_all(send_cache, "req", split_axis=0, concat_axis=0, tiled=True)
    prefill_partial = feed_forward_partial(prefill_res, mlp_gain, all_weights)
    _, recv_cache, recv_x = lax.optimization_barrier((prefill_partial, recv_cache, recv_x))
    prefill_out = feed_forward_finish(prefill_res, prefill_partial)
    arrival_rows = jnp.sum(jnp.where(chosen, (source * slot_total + slot_ids)[None, :], 0), axis=1)
    got_row = recv_x[arrival_rows]
    got_x = got_row[:, : decode_x.shape[1]]
    got_code = got_row[:, decode_x.shape[1] : decode_x.shape[1] + 2].astype(jnp.int32)
    got_length = got_code[:, 0] * 16 + got_code[:, 1]

    decode_q, decode_kv = project(
        rms_scale(got_x, attn_gain), inproj_weight, inproj_bias, got_length
    )
    cache_after, decode_att = decode_attend(
        arrival_order,
        got_length,
        recv_cache.reshape(n_req * CAP, cache_length, width_per_row),
        decode_kv,
        decode_q,
    )
    decode_res = got_x.astype(jnp.float32) + jnp.dot(
        decode_att, outproj_weight, preferred_element_type=jnp.float32
    )
    decode_out = small_feed_forward(decode_res, mlp_gain, all_weights)
    return (
        prefill_out[None, None],
        decode_out[None, None],
        cache_after[None, None],
    )


def feed_forward_partial(residual, mlp_gain, all_weights):
    mlp_in = rms_scale(residual, mlp_gain)
    gate_and_up = jnp.einsum(
        "nd,dkf->nkf",
        lax.all_gather(mlp_in, "blk", axis=0, tiled=True),
        all_weights[:, :2, :],
        preferred_element_type=jnp.float32,
    )
    hidden = (jax.nn.silu(gate_and_up[:, 0, :]) * gate_and_up[:, 1, :]).astype(jnp.bfloat16)
    return jnp.einsum(
        "nf,df->nd", hidden, all_weights[:, 2, :], preferred_element_type=jnp.float32
    ).astype(jnp.bfloat16)


def small_feed_forward(residual, mlp_gain, all_weights):
    n_blk = lax.axis_size("blk")
    rows = residual.shape[0]
    mlp_in = rms_scale(residual, mlp_gain)
    spread = jnp.broadcast_to(mlp_in[None], (n_blk,) + mlp_in.shape)
    gathered = lax.all_to_all(spread, "blk", split_axis=0, concat_axis=0, tiled=True)
    gate_and_up = jnp.einsum(
        "nd,dkf->nkf",
        gathered.reshape(n_blk * rows, -1),
        all_weights[:, :2, :],
        preferred_element_type=jnp.float32,
    )
    hidden = (jax.nn.silu(gate_and_up[:, 0, :]) * gate_and_up[:, 1, :]).astype(jnp.bfloat16)
    partial = jnp.einsum(
        "nf,df->nd", hidden, all_weights[:, 2, :], preferred_element_type=jnp.float32
    ).astype(jnp.bfloat16)
    returned = lax.all_to_all(
        partial.reshape(n_blk, rows, -1), "blk", split_axis=0, concat_axis=0, tiled=True
    )
    mlp_rows = jnp.sum(returned.astype(jnp.float32), axis=0)
    return (residual + mlp_rows).astype(jnp.bfloat16)


def feed_forward_finish(residual, partial):
    mlp_rows = lax.psum_scatter(partial, "blk", scatter_dimension=0, tiled=True)
    return (residual + mlp_rows.astype(jnp.float32)).astype(jnp.bfloat16)


def solution(mesh):
    return jax.shard_map(
        shards,
        mesh=mesh,
        in_specs=(
            P("blk", "req", None, None),
            P("blk", "req", None, None),
            P("blk", "req", None, None, None),
            P("blk", "req", None, None),
            P("blk", "req", None),
            P("blk", "req", None),
            P(),
            P(),
            P(),
            P(),
            P(),
            P("req", None, "blk"),
            P("blk", "req"),
        ),
        out_specs=(
            P("blk", "req", None, None),
            P("blk", "req", None, None),
            P("blk", "req", None, None, None),
        ),
        check_vma=False,
    )
```

```python
import math

import jax
import jax.numpy as jnp
from jax import lax
from jax.experimental import pallas as pl
from jax.experimental.pallas import tpu as pltpu
from jax.sharding import PartitionSpec as P

QUERY_HEADS = 12
KEY_VALUE_HEADS = 2
HEAD_SIZE = 128
CAP = 2


rms_eps = 1e-06
rope_base = 1000000.0


def rms_scale(rows, gain_row):
    rows_wide = rows.astype(jnp.float32)
    inverse = lax.rsqrt(jnp.mean(rows_wide * rows_wide, axis=-1, keepdims=True) + rms_eps)
    return (rows_wide * inverse * gain_row.astype(jnp.float32)).astype(jnp.bfloat16)


def apply_rotary(vectors, token_positions):
    head_dim = vectors.shape[-1]
    half_dim = head_dim // 2
    frequency = rope_base ** (-2.0 * jnp.arange(half_dim, dtype=jnp.float32) / head_dim)
    angles = token_positions.astype(jnp.float32)[:, None] * frequency[None, :]
    cosine = jnp.concatenate([jnp.cos(angles), jnp.cos(angles)], axis=-1)[:, None, :]
    sine_table = jnp.concatenate([jnp.sin(angles), jnp.sin(angles)], axis=-1)[:, None, :]
    turned = jnp.concatenate([-vectors[..., half_dim:], vectors[..., :half_dim]], axis=-1)
    return vectors * cosine + turned * sine_table


def project(normed, weight, bias_row, token_positions):
    mixed_batch = jnp.dot(normed, weight, preferred_element_type=jnp.float32) + bias_row.astype(
        jnp.float32
    )
    query_head_width = QUERY_HEADS * HEAD_SIZE
    key_head_width = KEY_VALUE_HEADS * HEAD_SIZE
    query_rows = apply_rotary(
        mixed_batch[:, :query_head_width].reshape(-1, QUERY_HEADS, HEAD_SIZE), token_positions
    )
    key_row_block = apply_rotary(
        mixed_batch[:, query_head_width : query_head_width + key_head_width].reshape(
            -1, KEY_VALUE_HEADS, HEAD_SIZE
        ),
        token_positions,
    )
    value_rows = mixed_batch[:, query_head_width + key_head_width :]
    key_value_pair = jnp.concatenate(
        [key_row_block.reshape(-1, key_head_width), value_rows], axis=-1
    )
    return (
        query_rows.reshape(-1, query_head_width).astype(jnp.bfloat16),
        key_value_pair.astype(jnp.bfloat16),
    )


def attend(query_rows, key_value_pair, allowed):
    batch_count = query_rows.shape[0]
    total_rows = query_rows.shape[1]
    group_width = QUERY_HEADS // KEY_VALUE_HEADS
    key_head_width = KEY_VALUE_HEADS * HEAD_SIZE
    grouped_heads = query_rows.reshape(
        batch_count, total_rows, KEY_VALUE_HEADS, group_width, HEAD_SIZE
    )
    key_row_block = key_value_pair[:, :, :key_head_width].reshape(
        batch_count, -1, KEY_VALUE_HEADS, HEAD_SIZE
    )
    value_rows = key_value_pair[:, :, key_head_width:].reshape(
        batch_count, -1, KEY_VALUE_HEADS, HEAD_SIZE
    )
    scores = jnp.einsum(
        "bqhgd,bkhd->bhgqk", grouped_heads, key_row_block, preferred_element_type=jnp.float32
    ) / math.sqrt(HEAD_SIZE)
    scores = jnp.where(allowed[:, None, None, :, :], scores, -jnp.inf)
    row_max = jnp.max(scores, axis=-1, keepdims=True)
    weights = jnp.exp(scores - row_max)
    weights = (weights / jnp.sum(weights, axis=-1, keepdims=True)).astype(jnp.bfloat16)
    result = jnp.einsum(
        "bhgqk,bkhd->bqhgd", weights, value_rows, preferred_element_type=jnp.float32
    )
    return result.reshape(batch_count, total_rows, QUERY_HEADS * HEAD_SIZE).astype(jnp.bfloat16)


def decode_kernel(order_ref, length_ref, first_ref, second_ref, kv_ref, q_ref, new_ref, att_ref):
    group_width = QUERY_HEADS // KEY_VALUE_HEADS
    key_head_width = KEY_VALUE_HEADS * HEAD_SIZE
    for half, cache_ref in enumerate((first_ref, second_ref)):
        limit = length_ref[2 * pl.program_id(0) + half]
        rows = cache_ref[...]
        positions = lax.broadcasted_iota(jnp.int32, rows.shape, 0)
        extended = jnp.where(
            positions < limit,
            rows,
            jnp.where(positions == limit, kv_ref[half], jnp.zeros_like(rows)),
        )
        new_ref[half] = extended
        key_ids = lax.broadcasted_iota(jnp.int32, (group_width, rows.shape[0]), 1)
        for head in range(KEY_VALUE_HEADS):
            keys = extended[:, head * HEAD_SIZE : (head + 1) * HEAD_SIZE]
            values = extended[
                :, key_head_width + head * HEAD_SIZE : key_head_width + (head + 1) * HEAD_SIZE
            ]
            scores = lax.dot_general(
                q_ref[half, head], keys, (((1,), (1,)), ((), ())), preferred_element_type=jnp.float32
            ) / math.sqrt(HEAD_SIZE)
            scores = jnp.where(key_ids <= limit, scores, -jnp.inf)
            weights = jnp.exp(scores - jnp.max(scores, axis=1, keepdims=True))
            weights = (weights / jnp.sum(weights, axis=1, keepdims=True)).astype(jnp.bfloat16)
            att_ref[half, head] = jnp.dot(
                weights, values, preferred_element_type=jnp.float32
            ).astype(jnp.bfloat16)


def decode_attend(arrival_order, got_length, recv_cache, decode_kv, decode_q):
    count = arrival_order.shape[0]
    cache_length, width_per_row = recv_cache.shape[1:]
    group_width = QUERY_HEADS // KEY_VALUE_HEADS
    order = jnp.clip(arrival_order, 0, recv_cache.shape[0] - 1)
    head_block = (2, KEY_VALUE_HEADS, group_width, HEAD_SIZE)
    new_cache, attended = pl.pallas_call(
        decode_kernel,
        grid_spec=pltpu.PrefetchScalarGridSpec(
            num_scalar_prefetch=2,
            grid=(count // 2,),
            in_specs=[
                pl.BlockSpec((None, cache_length, width_per_row), lambda p, o, n: (o[2 * p], 0, 0)),
                pl.BlockSpec(
                    (None, cache_length, width_per_row), lambda p, o, n: (o[2 * p + 1], 0, 0)
                ),
                pl.BlockSpec((2, 1, width_per_row), lambda p, o, n: (p, 0, 0)),
                pl.BlockSpec(head_block, lambda p, o, n: (p, 0, 0, 0)),
            ],
            out_specs=[
                pl.BlockSpec((2, cache_length, width_per_row), lambda p, o, n: (p, 0, 0)),
                pl.BlockSpec(head_block, lambda p, o, n: (p, 0, 0, 0)),
            ],
        ),
        out_shape=[
            jax.ShapeDtypeStruct((count, cache_length, width_per_row), jnp.bfloat16),
            jax.ShapeDtypeStruct((count, KEY_VALUE_HEADS, group_width, HEAD_SIZE), jnp.bfloat16),
        ],
    )(
        order,
        got_length,
        recv_cache,
        recv_cache,
        decode_kv.reshape(count, 1, width_per_row),
        decode_q.reshape(count, KEY_VALUE_HEADS, group_width, HEAD_SIZE),
    )
    return new_cache, attended.reshape(count, QUERY_HEADS * HEAD_SIZE)


def extend(cache_rows, key_value_pair, lengths_now):
    token_positions = jnp.arange(cache_rows.shape[1], dtype=jnp.int32)[None, :, None]
    limit = lengths_now[:, None, None]
    return jnp.where(
        token_positions < limit,
        cache_rows,
        jnp.where(token_positions == limit, key_value_pair[:, None, :], jnp.zeros_like(cache_rows)),
    )


def shards(
    prefill_rows,
    decode_rows,
    cache_pool,
    page_table,
    lengths,
    destination,
    attn_gain,
    inproj_weight,
    inproj_bias,
    outproj_weight,
    mlp_gain,
    gate_up,
    down_weight,
):
    n_req = lax.axis_size("req")
    own_index = lax.axis_index("req")
    slot_total = destination.shape[2]
    pool_rows = cache_pool[0, 0]
    table_rows = page_table[0, 0]
    width_per_row = pool_rows.shape[-1]
    cache_length = table_rows.shape[1] * pool_rows.shape[1]
    context = pool_rows[table_rows[slot_total]].reshape(cache_length, width_per_row)
    context_length = lengths[0, 0, slot_total]
    slot_ids = jnp.arange(slot_total, dtype=jnp.int32)

    local_down = jnp.transpose(down_weight)[:, None, :]
    all_weights = lax.all_gather(
        jnp.concatenate([gate_up, local_down], axis=1), "req", axis=0, tiled=True
    )

    send_dest = destination[0, 0]
    decode_x = decode_rows[0, 0]
    own_len = lengths[0, 0, :slot_total]
    same_dest = send_dest[None, :] == send_dest[:, None]
    earlier = same_dest & (slot_ids[None, :] < slot_ids[:, None])
    within = jnp.sum(earlier.astype(jnp.int32), axis=1)
    target = send_dest * CAP + within
    flat_slots = jnp.arange(n_req * CAP, dtype=jnp.int32)
    matches = target[None, :] == flat_slots[:, None]
    picked = jnp.sum(jnp.where(matches, slot_ids[None, :], 0), axis=1)
    send_pages = table_rows[picked]
    send_cache = pool_rows[send_pages].reshape(n_req, CAP, cache_length, width_per_row)
    sent_len = own_len[picked]
    length_code = jnp.stack([sent_len // 16, sent_len % 16], axis=1).astype(jnp.bfloat16)
    send_x = jnp.concatenate(
        [decode_x[picked], jnp.pad(length_code, ((0, 0), (0, 126)))], axis=1
    ).reshape(n_req, CAP, -1)

    shift = jnp.mod(send_dest - own_index, n_req)
    source = jnp.mod(own_index - shift, n_req)
    order_key = source * slot_total + slot_ids
    rank = jnp.sum((order_key[None, :] < order_key[:, None]).astype(jnp.int32), axis=1)
    chosen = rank[None, :] == slot_ids[:, None]
    arrival_order = jnp.sum(jnp.where(chosen, (source * CAP + within)[None, :], 0), axis=1)

    prefill_x = prefill_rows[0, 0]
    prefill_count = prefill_x.shape[0]
    block_ids = jnp.arange(prefill_count, dtype=jnp.int32)
    cache_ids = jnp.arange(cache_length, dtype=jnp.int32)
    prefill_q, prefill_kv = project(
        rms_scale(prefill_x, attn_gain), inproj_weight, inproj_bias, context_length + block_ids
    )
    key_block = jnp.concatenate([context, prefill_kv], axis=0)
    allowed = jnp.concatenate(
        [
            jnp.broadcast_to(cache_ids[None, :] < context_length, (prefill_count, cache_length)),
            block_ids[None, :] <= block_ids[:, None],
        ],
        axis=1,
    )
    prefill_att = attend(prefill_q[None], key_block[None], allowed[None])[0]
    prefill_res = prefill_x.astype(jnp.float32) + jnp.dot(
        prefill_att, outproj_weight, preferred_element_type=jnp.float32
    )
    all_weights, prefill_res, send_cache = lax.optimization_barrier(
        (all_weights, prefill_res, send_cache)
    )
    recv_cache = lax.all_to_all(send_cache, "req", split_axis=0, concat_axis=0, tiled=True)
    prefill_partial = feed_forward_partial(prefill_res, mlp_gain, all_weights)
    _, recv_cache, send_x = lax.optimization_barrier((prefill_partial, recv_cache, send_x))
    recv_x = lax.all_to_all(send_x, "req", split_axis=0, concat_axis=0, tiled=True)
    prefill_out = feed_forward_finish(prefill_res, prefill_partial)
    got_row = recv_x.reshape(n_req * CAP, -1)[arrival_order]
    got_x = got_row[:, : decode_x.shape[1]]
    got_code = got_row[:, decode_x.shape[1] : decode_x.shape[1] + 2].astype(jnp.int32)
    got_length = got_code[:, 0] * 16 + got_code[:, 1]

    decode_q, decode_kv = project(
        rms_scale(got_x, attn_gain), inproj_weight, inproj_bias, got_length
    )
    cache_after, decode_att = decode_attend(
        arrival_order,
        got_length,
        recv_cache.reshape(n_req * CAP, cache_length, width_per_row),
        decode_kv,
        decode_q,
    )
    decode_res = got_x.astype(jnp.float32) + jnp.dot(
        decode_att, outproj_weight, preferred_element_type=jnp.float32
    )
    decode_out = small_feed_forward(decode_res, mlp_gain, all_weights)
    return (
        prefill_out[None, None],
        decode_out[None, None],
        cache_after[None, None],
    )


def feed_forward_partial(residual, mlp_gain, all_weights):
    mlp_in = rms_scale(residual, mlp_gain)
    gate_and_up = jnp.einsum(
        "nd,dkf->nkf",
        lax.all_gather(mlp_in, "blk", axis=0, tiled=True),
        all_weights[:, :2, :],
        preferred_element_type=jnp.float32,
    )
    hidden = (jax.nn.silu(gate_and_up[:, 0, :]) * gate_and_up[:, 1, :]).astype(jnp.bfloat16)
    return jnp.einsum(
        "nf,df->nd", hidden, all_weights[:, 2, :], preferred_element_type=jnp.float32
    ).astype(jnp.bfloat16)


def small_feed_forward(residual, mlp_gain, all_weights):
    n_blk = lax.axis_size("blk")
    rows = residual.shape[0]
    mlp_in = rms_scale(residual, mlp_gain)
    spread = jnp.broadcast_to(mlp_in[None], (n_blk,) + mlp_in.shape)
    gathered = lax.all_to_all(spread, "blk", split_axis=0, concat_axis=0, tiled=True)
    gate_and_up = jnp.einsum(
        "nd,dkf->nkf",
        gathered.reshape(n_blk * rows, -1),
        all_weights[:, :2, :],
        preferred_element_type=jnp.float32,
    )
    hidden = (jax.nn.silu(gate_and_up[:, 0, :]) * gate_and_up[:, 1, :]).astype(jnp.bfloat16)
    partial = jnp.einsum(
        "nf,df->nd", hidden, all_weights[:, 2, :], preferred_element_type=jnp.float32
    ).astype(jnp.bfloat16)
    returned = lax.all_to_all(
        partial.reshape(n_blk, rows, -1), "blk", split_axis=0, concat_axis=0, tiled=True
    )
    mlp_rows = jnp.sum(returned.astype(jnp.float32), axis=0)
    return (residual + mlp_rows).astype(jnp.bfloat16)


def feed_forward_finish(residual, partial):
    mlp_rows = lax.psum_scatter(partial, "blk", scatter_dimension=0, tiled=True)
    return (residual + mlp_rows.astype(jnp.float32)).astype(jnp.bfloat16)


def solution(mesh):
    return jax.shard_map(
        shards,
        mesh=mesh,
        in_specs=(
            P("blk", "req", None, None),
            P("blk", "req", None, None),
            P("blk", "req", None, None, None),
            P("blk", "req", None, None),
            P("blk", "req", None),
            P("blk", "req", None),
            P(),
            P(),
            P(),
            P(),
            P(),
            P("req", None, "blk"),
            P("blk", "req"),
        ),
        out_specs=(
            P("blk", "req", None, None),
            P("blk", "req", None, None),
            P("blk", "req", None, None, None),
        ),
        check_vma=False,
    )
```

```python
import math

import jax
import jax.numpy as jnp
from jax import lax
from jax.experimental import pallas as pl
from jax.experimental.pallas import tpu as pltpu
from jax.sharding import PartitionSpec as P

QUERY_HEADS = 12
KEY_VALUE_HEADS = 2
HEAD_SIZE = 128
CAP = 2
PER_STEP = 4


rms_eps = 1e-06
rope_base = 1000000.0


def rms_scale(rows, gain_row):
    rows_wide = rows.astype(jnp.float32)
    inverse = lax.rsqrt(jnp.mean(rows_wide * rows_wide, axis=-1, keepdims=True) + rms_eps)
    return (rows_wide * inverse * gain_row.astype(jnp.float32)).astype(jnp.bfloat16)


def apply_rotary(vectors, token_positions):
    head_dim = vectors.shape[-1]
    half_dim = head_dim // 2
    frequency = rope_base ** (-2.0 * jnp.arange(half_dim, dtype=jnp.float32) / head_dim)
    angles = token_positions.astype(jnp.float32)[:, None] * frequency[None, :]
    cosine = jnp.concatenate([jnp.cos(angles), jnp.cos(angles)], axis=-1)[:, None, :]
    sine_table = jnp.concatenate([jnp.sin(angles), jnp.sin(angles)], axis=-1)[:, None, :]
    turned = jnp.concatenate([-vectors[..., half_dim:], vectors[..., :half_dim]], axis=-1)
    return vectors * cosine + turned * sine_table


def project(normed, weight, bias_row, token_positions):
    mixed_batch = jnp.dot(normed, weight, preferred_element_type=jnp.float32) + bias_row.astype(
        jnp.float32
    )
    query_head_width = QUERY_HEADS * HEAD_SIZE
    key_head_width = KEY_VALUE_HEADS * HEAD_SIZE
    query_rows = apply_rotary(
        mixed_batch[:, :query_head_width].reshape(-1, QUERY_HEADS, HEAD_SIZE), token_positions
    )
    key_row_block = apply_rotary(
        mixed_batch[:, query_head_width : query_head_width + key_head_width].reshape(
            -1, KEY_VALUE_HEADS, HEAD_SIZE
        ),
        token_positions,
    )
    value_rows = mixed_batch[:, query_head_width + key_head_width :]
    key_value_pair = jnp.concatenate(
        [key_row_block.reshape(-1, key_head_width), value_rows], axis=-1
    )
    return (
        query_rows.reshape(-1, query_head_width).astype(jnp.bfloat16),
        key_value_pair.astype(jnp.bfloat16),
    )


def attend(query_rows, key_value_pair, allowed):
    batch_count = query_rows.shape[0]
    total_rows = query_rows.shape[1]
    group_width = QUERY_HEADS // KEY_VALUE_HEADS
    key_head_width = KEY_VALUE_HEADS * HEAD_SIZE
    grouped_heads = query_rows.reshape(
        batch_count, total_rows, KEY_VALUE_HEADS, group_width, HEAD_SIZE
    )
    key_row_block = key_value_pair[:, :, :key_head_width].reshape(
        batch_count, -1, KEY_VALUE_HEADS, HEAD_SIZE
    )
    value_rows = key_value_pair[:, :, key_head_width:].reshape(
        batch_count, -1, KEY_VALUE_HEADS, HEAD_SIZE
    )
    scores = jnp.einsum(
        "bqhgd,bkhd->bhgqk", grouped_heads, key_row_block, preferred_element_type=jnp.float32
    ) / math.sqrt(HEAD_SIZE)
    scores = jnp.where(allowed[:, None, None, :, :], scores, -jnp.inf)
    row_max = jnp.max(scores, axis=-1, keepdims=True)
    weights = jnp.exp(scores - row_max)
    weights = (weights / jnp.sum(weights, axis=-1, keepdims=True)).astype(jnp.bfloat16)
    result = jnp.einsum(
        "bhgqk,bkhd->bqhgd", weights, value_rows, preferred_element_type=jnp.float32
    )
    return result.reshape(batch_count, total_rows, QUERY_HEADS * HEAD_SIZE).astype(jnp.bfloat16)


def decode_kernel(order_ref, length_ref, *refs):
    cache_refs = refs[:PER_STEP]
    kv_ref, q_ref, new_ref, att_ref = refs[PER_STEP:]
    group_width = QUERY_HEADS // KEY_VALUE_HEADS
    key_head_width = KEY_VALUE_HEADS * HEAD_SIZE
    for half, cache_ref in enumerate(cache_refs):
        limit = length_ref[PER_STEP * pl.program_id(0) + half]
        rows = cache_ref[...]
        positions = lax.broadcasted_iota(jnp.int32, rows.shape, 0)
        extended = jnp.where(
            positions < limit,
            rows,
            jnp.where(positions == limit, kv_ref[half], jnp.zeros_like(rows)),
        )
        new_ref[half] = extended
        key_ids = lax.broadcasted_iota(jnp.int32, (group_width, rows.shape[0]), 1)
        for head in range(KEY_VALUE_HEADS):
            keys = extended[:, head * HEAD_SIZE : (head + 1) * HEAD_SIZE]
            values = extended[
                :, key_head_width + head * HEAD_SIZE : key_head_width + (head + 1) * HEAD_SIZE
            ]
            scores = lax.dot_general(
                q_ref[half, head], keys, (((1,), (1,)), ((), ())), preferred_element_type=jnp.float32
            ) / math.sqrt(HEAD_SIZE)
            scores = jnp.where(key_ids <= limit, scores, -jnp.inf)
            weights = jnp.exp(scores - jnp.max(scores, axis=1, keepdims=True))
            weights = (weights / jnp.sum(weights, axis=1, keepdims=True)).astype(jnp.bfloat16)
            att_ref[half, head] = jnp.dot(
                weights, values, preferred_element_type=jnp.float32
            ).astype(jnp.bfloat16)


def decode_attend(arrival_order, got_length, recv_cache, decode_kv, decode_q):
    count = arrival_order.shape[0]
    cache_length, width_per_row = recv_cache.shape[1:]
    group_width = QUERY_HEADS // KEY_VALUE_HEADS
    order = jnp.clip(arrival_order, 0, recv_cache.shape[0] - 1)
    head_block = (PER_STEP, KEY_VALUE_HEADS, group_width, HEAD_SIZE)
    new_cache, attended = pl.pallas_call(
        decode_kernel,
        grid_spec=pltpu.PrefetchScalarGridSpec(
            num_scalar_prefetch=2,
            grid=(count // PER_STEP,),
            in_specs=[
                *[
                    pl.BlockSpec(
                        (None, cache_length, width_per_row),
                        lambda p, o, n, k=k: (o[PER_STEP * p + k], 0, 0),
                    )
                    for k in range(PER_STEP)
                ],
                pl.BlockSpec((PER_STEP, 1, width_per_row), lambda p, o, n: (p, 0, 0)),
                pl.BlockSpec(head_block, lambda p, o, n: (p, 0, 0, 0)),
            ],
            out_specs=[
                pl.BlockSpec((PER_STEP, cache_length, width_per_row), lambda p, o, n: (p, 0, 0)),
                pl.BlockSpec(head_block, lambda p, o, n: (p, 0, 0, 0)),
            ],
        ),
        out_shape=[
            jax.ShapeDtypeStruct((count, cache_length, width_per_row), jnp.bfloat16),
            jax.ShapeDtypeStruct((count, KEY_VALUE_HEADS, group_width, HEAD_SIZE), jnp.bfloat16),
        ],
    )(
        order,
        got_length,
        *([recv_cache] * PER_STEP),
        decode_kv.reshape(count, 1, width_per_row),
        decode_q.reshape(count, KEY_VALUE_HEADS, group_width, HEAD_SIZE),
    )
    return new_cache, attended.reshape(count, QUERY_HEADS * HEAD_SIZE)


def extend(cache_rows, key_value_pair, lengths_now):
    token_positions = jnp.arange(cache_rows.shape[1], dtype=jnp.int32)[None, :, None]
    limit = lengths_now[:, None, None]
    return jnp.where(
        token_positions < limit,
        cache_rows,
        jnp.where(token_positions == limit, key_value_pair[:, None, :], jnp.zeros_like(cache_rows)),
    )


def shards(
    prefill_rows,
    decode_rows,
    cache_pool,
    page_table,
    lengths,
    destination,
    attn_gain,
    inproj_weight,
    inproj_bias,
    outproj_weight,
    mlp_gain,
    gate_up,
    down_weight,
):
    n_req = lax.axis_size("req")
    own_index = lax.axis_index("req")
    slot_total = destination.shape[2]
    pool_rows = cache_pool[0, 0]
    table_rows = page_table[0, 0]
    width_per_row = pool_rows.shape[-1]
    cache_length = table_rows.shape[1] * pool_rows.shape[1]
    context = pool_rows[table_rows[slot_total]].reshape(cache_length, width_per_row)
    context_length = lengths[0, 0, slot_total]
    slot_ids = jnp.arange(slot_total, dtype=jnp.int32)

    local_down = jnp.transpose(down_weight)[:, None, :]
    all_weights = lax.all_gather(
        jnp.concatenate([gate_up, local_down], axis=1), "req", axis=0, tiled=True
    )

    send_dest = destination[0, 0]
    decode_x = decode_rows[0, 0]
    own_len = lengths[0, 0, :slot_total]
    same_dest = send_dest[None, :] == send_dest[:, None]
    earlier = same_dest & (slot_ids[None, :] < slot_ids[:, None])
    within = jnp.sum(earlier.astype(jnp.int32), axis=1)
    target = send_dest * CAP + within
    flat_slots = jnp.arange(n_req * CAP, dtype=jnp.int32)
    matches = target[None, :] == flat_slots[:, None]
    picked = jnp.sum(jnp.where(matches, slot_ids[None, :], 0), axis=1)
    send_pages = table_rows[picked]
    send_cache = pool_rows[send_pages].reshape(n_req, CAP, cache_length, width_per_row)
    sent_len = own_len[picked]
    length_code = jnp.stack([sent_len // 16, sent_len % 16], axis=1).astype(jnp.bfloat16)
    send_x = jnp.concatenate(
        [decode_x[picked], jnp.pad(length_code, ((0, 0), (0, 126)))], axis=1
    ).reshape(n_req, CAP, -1)
    recv_x = lax.all_to_all(send_x, "req", split_axis=0, concat_axis=0, tiled=True)

    shift = jnp.mod(send_dest - own_index, n_req)
    source = jnp.mod(own_index - shift, n_req)
    order_key = source * slot_total + slot_ids
    rank = jnp.sum((order_key[None, :] < order_key[:, None]).astype(jnp.int32), axis=1)
    chosen = rank[None, :] == slot_ids[:, None]
    arrival_order = jnp.sum(jnp.where(chosen, (source * CAP + within)[None, :], 0), axis=1)

    prefill_x = prefill_rows[0, 0]
    prefill_count = prefill_x.shape[0]
    block_ids = jnp.arange(prefill_count, dtype=jnp.int32)
    cache_ids = jnp.arange(cache_length, dtype=jnp.int32)
    prefill_q, prefill_kv = project(
        rms_scale(prefill_x, attn_gain), inproj_weight, inproj_bias, context_length + block_ids
    )
    key_block = jnp.concatenate([context, prefill_kv], axis=0)
    allowed = jnp.concatenate(
        [
            jnp.broadcast_to(cache_ids[None, :] < context_length, (prefill_count, cache_length)),
            block_ids[None, :] <= block_ids[:, None],
        ],
        axis=1,
    )
    prefill_att = attend(prefill_q[None], key_block[None], allowed[None])[0]
    prefill_res = prefill_x.astype(jnp.float32) + jnp.dot(
        prefill_att, outproj_weight, preferred_element_type=jnp.float32
    )
    all_weights, prefill_res, send_cache = lax.optimization_barrier(
        (all_weights, prefill_res, send_cache)
    )
    recv_cache = lax.all_to_all(send_cache, "req", split_axis=0, concat_axis=0, tiled=True)
    prefill_partial = feed_forward_partial(prefill_res, mlp_gain, all_weights)
    _, recv_cache, recv_x = lax.optimization_barrier((prefill_partial, recv_cache, recv_x))
    prefill_out = feed_forward_finish(prefill_res, prefill_partial)
    got_row = recv_x.reshape(n_req * CAP, -1)[arrival_order]
    got_x = got_row[:, : decode_x.shape[1]]
    got_code = got_row[:, decode_x.shape[1] : decode_x.shape[1] + 2].astype(jnp.int32)
    got_length = got_code[:, 0] * 16 + got_code[:, 1]

    decode_q, decode_kv = project(
        rms_scale(got_x, attn_gain), inproj_weight, inproj_bias, got_length
    )
    cache_after, decode_att = decode_attend(
        arrival_order,
        got_length,
        recv_cache.reshape(n_req * CAP, cache_length, width_per_row),
        decode_kv,
        decode_q,
    )
    decode_res = got_x.astype(jnp.float32) + jnp.dot(
        decode_att, outproj_weight, preferred_element_type=jnp.float32
    )
    decode_out = small_feed_forward(decode_res, mlp_gain, all_weights)
    return (
        prefill_out[None, None],
        decode_out[None, None],
        cache_after[None, None],
    )


def feed_forward_partial(residual, mlp_gain, all_weights):
    mlp_in = rms_scale(residual, mlp_gain)
    gate_and_up = jnp.einsum(
        "nd,dkf->nkf",
        lax.all_gather(mlp_in, "blk", axis=0, tiled=True),
        all_weights[:, :2, :],
        preferred_element_type=jnp.float32,
    )
    hidden = (jax.nn.silu(gate_and_up[:, 0, :]) * gate_and_up[:, 1, :]).astype(jnp.bfloat16)
    return jnp.einsum(
        "nf,df->nd", hidden, all_weights[:, 2, :], preferred_element_type=jnp.float32
    ).astype(jnp.bfloat16)


def small_feed_forward(residual, mlp_gain, all_weights):
    n_blk = lax.axis_size("blk")
    rows = residual.shape[0]
    mlp_in = rms_scale(residual, mlp_gain)
    spread = jnp.broadcast_to(mlp_in[None], (n_blk,) + mlp_in.shape)
    gathered = lax.all_to_all(spread, "blk", split_axis=0, concat_axis=0, tiled=True)
    gate_and_up = jnp.einsum(
        "nd,dkf->nkf",
        gathered.reshape(n_blk * rows, -1),
        all_weights[:, :2, :],
        preferred_element_type=jnp.float32,
    )
    hidden = (jax.nn.silu(gate_and_up[:, 0, :]) * gate_and_up[:, 1, :]).astype(jnp.bfloat16)
    partial = jnp.einsum(
        "nf,df->nd", hidden, all_weights[:, 2, :], preferred_element_type=jnp.float32
    ).astype(jnp.bfloat16)
    returned = lax.all_to_all(
        partial.reshape(n_blk, rows, -1), "blk", split_axis=0, concat_axis=0, tiled=True
    )
    mlp_rows = jnp.sum(returned.astype(jnp.float32), axis=0)
    return (residual + mlp_rows).astype(jnp.bfloat16)


def feed_forward_finish(residual, partial):
    mlp_rows = lax.psum_scatter(partial, "blk", scatter_dimension=0, tiled=True)
    return (residual + mlp_rows.astype(jnp.float32)).astype(jnp.bfloat16)


def solution(mesh):
    return jax.shard_map(
        shards,
        mesh=mesh,
        in_specs=(
            P("blk", "req", None, None),
            P("blk", "req", None, None),
            P("blk", "req", None, None, None),
            P("blk", "req", None, None),
            P("blk", "req", None),
            P("blk", "req", None),
            P(),
            P(),
            P(),
            P(),
            P(),
            P("req", None, "blk"),
            P("blk", "req"),
        ),
        out_specs=(
            P("blk", "req", None, None),
            P("blk", "req", None, None),
            P("blk", "req", None, None, None),
        ),
        check_vma=False,
    )
```
